256 devices in a mesh: dp: 4 (over x_hi, core), sx: 8 (over y, x_lo), syz: 8 (over z).
Axes of the slice: x: 4 (x_hi: 2, x_lo: 2; x = x_hi * 2 + x_lo), y: 4, z: 8, core: 2. Of those that a mesh axis runs over, the one named last changes fastest.
Arguments:
- input_act: bfloat16 [4, 32, 128, 64, 128], P('dp', 'sx', 'syz'), may hold values from -6 to 6
- pre_act: bfloat16 [4, 16, 64, 64, 128], P('dp', 'sx', 'syz'), may hold values from -6 to 6
- out_grad: bfloat16 [4, 8, 32, 32, 128], P('dp', 'sx', 'syz'), may hold values from -24 to 24
- weight_one: bfloat16 [3, 3, 3, 64, 128], replicated, may hold values from -0.15625 to 0.15625
- weight_two: bfloat16 [3, 3, 3, 128, 128], replicated, may hold values from -0.109375 to 0.109375
Outputs:
- grad_input: bfloat16 [4, 32, 128, 64, 128], P('dp', 'sx', 'syz')
- grad_one: float32 [3, 3, 3, 64, 128], replicated
- grad_two: float32 [3, 3, 3, 128, 128], replicated
The draws below stay inside these ranges and needn't reach their ends.
All inputs are finite; a program needn't handle non-finite values.
Results may differ from the reference program's by a relative error of at most 0.0049.
Values may be sent and summed in bfloat16 or wider, within the bound.
No kernel may reach another device: no remote copies, remote signals or barrier semaphores. Data moves between devices by JAX's collectives and lax.ppermute only.
A program may use at most 64 MiB of HBM per device.

```python
import jax
import jax.numpy as jnp
from jax import lax

CIN = 64
C1 = 128
C2 = 128
Z0 = 128
NVOL = 4
NX0 = 32
NY0 = 128


def levels(own_key, extent, split, least, top_value):
    gain = 1.0
    for axis_at, parts in split:
        heights = jax.random.uniform(jax.random.fold_in(jax.random.fold_in(own_key, 6), axis_at), (parts,), jnp.float32, least / len(split), top_value / len(split))
        gain = gain * jnp.repeat(jnp.exp(heights), extent[axis_at] // parts).reshape((-1,) + (1,) * (len(extent) - 1 - axis_at))
    return gain


def centred(key, shape, spread, most, split=(), dtype=jnp.bfloat16):
    gain = levels(key, shape, split, -0.22, 0.18) if split else 1.0
    entries = jax.random.normal(key, shape, jnp.float32) * spread * gain
    return jnp.minimum(jnp.maximum(entries, -most), most).astype(dtype)


def setup_inputs(seed: int = 0) -> dict:
    splits = jax.random.split(jax.random.key(seed), 6)
    input_act = centred(splits[0], (NVOL, NX0, NY0, Z0 // 2, 2 * CIN), 1.0, 6.0, ((0, 4), (1, 8), (2, 8)))
    pre_act = centred(splits[1], (NVOL, NX0 // 2, NY0 // 2, Z0 // 2, C1), 1.0, 6.0, ((0, 4), (1, 8), (2, 8)))
    out_grad = centred(splits[2], (NVOL, NX0 // 4, NY0 // 4, Z0 // 4, C2), 4.0, 24.0, ((0, 4), (1, 8), (2, 8)))
    weight_one = centred(splits[3], (3, 3, 3, CIN, C1), (27 * CIN) ** -0.5, 0.15625)
    weight_two = centred(splits[4], (3, 3, 3, C1, C2), (27 * C1) ** -0.5, 0.109375)
    return dict(input_act=input_act, pre_act=pre_act, out_grad=out_grad, weight_one=weight_one, weight_two=weight_two)


def strided(field, kernel):
    return lax.conv_general_dilated(field, kernel, (2, 2, 2), ((1, 1), (1, 1), (1, 1)), dimension_numbers=('NDHWC', 'DHWIO', 'NDHWC'), precision=lax.Precision.HIGHEST)

def reference(input_act, pre_act, out_grad, weight_one, weight_two):
    kernel_one = weight_one.astype(jnp.float32)
    kernel_two = weight_two.astype(jnp.float32)

    def one_volume(items):
        volume_in, volume_pre, volume_grad = items
        size_x, size_y, size_p, _ = volume_in.shape
        natural = volume_in.astype(jnp.float32).reshape(size_x, size_y, 2 * size_p, CIN)[None]
        pre_float = volume_pre.astype(jnp.float32)
        activation = jnp.where(pre_float > 0, pre_float, 0.3 * pre_float).astype(jnp.bfloat16)
        activation = lax.optimization_barrier(activation).astype(jnp.float32)
        _, back_two = jax.vjp(strided, activation[None], kernel_two)
        grad_act, weight_grad_two = back_two(volume_grad.astype(jnp.float32)[None])
        grad_pre = (grad_act[0] * jnp.where(pre_float > 0, 1.0, 0.3)).astype(jnp.bfloat16)
        grad_pre = lax.optimization_barrier(grad_pre).astype(jnp.float32)
        _, back_one = jax.vjp(strided, natural, kernel_one)
        grad_in, weight_grad_one = back_one(grad_pre[None])
        grad_in = grad_in[0].reshape(size_x, size_y, size_p, 2 * CIN).astype(jnp.bfloat16)
        return (grad_in, weight_grad_one, weight_grad_two)
    grad_input, grads_one, grads_two = lax.map(one_volume, (input_act, pre_act, out_grad))
    scale_one = float(NVOL * (NX0 // 2) * (NY0 // 2) * (Z0 // 2)) ** (-0.5)
    scale_two = float(NVOL * (NX0 // 4) * (NY0 // 4) * (Z0 // 4)) ** (-0.5)
    grad_one = lax.optimization_barrier(jnp.sum(grads_one, axis=0)) * scale_one
    grad_two = lax.optimization_barrier(jnp.sum(grads_two, axis=0)) * scale_two
    return (grad_input, grad_one, grad_two)
```

```python
import functools

import jax
import jax.numpy as jnp
from jax import lax
from jax.experimental import pallas as pl
from jax.experimental.pallas import tpu as pltpu
from jax.sharding import Mesh
from jax.sharding import PartitionSpec as P

BF = jnp.bfloat16
F32 = jnp.float32

CX, CY, CZ = 1, 4, 32
MX, MY, MZ = 2, 8, 64
CIN, C1, C2 = 64, 128, 128
EX, EY = MX + 1, MY + 1
CHUNK = 88
GROUP = 32
HALF = CHUNK * GROUP
ROWS_ONE = 27 * CIN
ROWS_TWO = 27 * C1
ROWS = 2 * HALF
SCALE_ONE = float(4 * 16 * 64 * 64) ** (-0.5)
SCALE_TWO = float(4 * 8 * 32 * 32) ** (-0.5)

TAP = ((1, 1), (0, 0), (1, 0))
TAPS = (((1, 0),), ((2, 0), (0, 1)))
SLOT = (2, 0, 1)


def nt(a, b):
    return lax.dot_general(a, b, (((1,), (1,)), ((), ())), preferred_element_type=F32)


def nn(a, b):
    return lax.dot_general(a, b, (((1,), (0,)), ((), ())), preferred_element_type=F32)


def next_row(value, period):
    rows = value.shape[0]
    rolled = pltpu.roll(value, rows - 1, 0)
    row = lax.broadcasted_iota(jnp.int32, value.shape, 0)
    return jnp.where(row % period == period - 1, 0.0, rolled)


def main_kernel(
    core_ref, u_ref, pre_ref, og_ref, hx_ref, hy_ref, hc_ref, w1_ref, w2_ref,
    a_ref, keep_ref, send_ref,
    b_s, r2_s, ga_s, act_s, u2t_s, u1t_s, buf_s,
):
    zero = jnp.zeros((C1, C2), BF)
    for kx in range(3):
        for ky in range(3):
            t = kx * 3 + ky
            r2_s[t, 0:C1, 0:C2] = w2_ref[kx, ky, 1]
            r2_s[t, 0:C1, C2:] = zero
            r2_s[t, C1:, 0:C2] = w2_ref[kx, ky, 2]
            r2_s[t, C1:, C2:] = w2_ref[kx, ky, 0]

    def put_b(at, value):
        n = value.shape[0]
        b_s[at : at + n, 0:C2] = value
        b_s[at : at + n, C2:] = next_row(value.astype(F32), CZ).astype(BF)

    put_b(0, og_ref[0, 0].reshape(CY * CZ, C2))
    put_b(CY * CZ, hy_ref[0:CZ])
    put_b((CY + 1) * CZ, hx_ref[0 : CY * CZ])
    put_b((2 * CY + 1) * CZ, hc_ref[0:CZ])

    def put_ga(mx, my, value):
        base = (mx * EY + my) * MZ
        ga_s[pl.ds(base, CZ, stride=2), :] = value[:, 0:C1]
        ga_s[pl.ds(base + 1, CZ, stride=2), :] = value[:, C1:]

    def b_rows(i, j, n):
        at = (i * (CY + 1) + j) * CZ
        return b_s[at : at + n * CZ, :]

    for px in range(2):
        for i in range(2 - px):
            for py in range(2):
                n = CY + 1 - py
                total = None
                for kx, dx in TAPS[px]:
                    for ky, dy in TAPS[py]:
                        part = nt(b_rows(i + dx, dy, n), r2_s[kx * 3 + ky])
                        total = part if total is None else total + part
                for j in range(n):
                    put_ga(2 * i + px, 2 * j + py, total[j * CZ : (j + 1) * CZ])

    def put_a(at, pre):
        n = pre.shape[0]
        slope = jnp.where(pre.astype(F32) > 0, 1.0, 0.3)
        value = ga_s[at : at + n, :] * slope
        a_ref[at : at + n, 0:C1] = value.astype(BF)
        a_ref[at : at + n, C1:] = next_row(value, MZ).astype(BF)

    own = MY * MZ
    for mx in range(MX):
        put_a(mx * EY * MZ, pre_ref[0, mx].reshape(own, C1))
        put_a((mx * EY + MY) * MZ, hy_ref[CZ + mx * MZ : CZ + (mx + 1) * MZ])
    put_a(MX * EY * MZ, hx_ref[CY * CZ : CY * CZ + own])
    put_a((MX * EY + MY) * MZ, hc_ref[CZ : CZ + MZ])

    for mx in range(MX):
        pre = pre_ref[0, mx].reshape(own, C1).astype(F32)
        act_s[mx * own : (mx + 1) * own, :] = jnp.where(pre > 0, pre, 0.3 * pre)
    for px in range(2):
        for py in range(2):
            for s in range(2):
                rows = [
                    act_s[pl.ds((px * MY + 2 * j + py) * MZ + s, CZ, stride=2), :]
                    for j in range(CY)
                ]
                u2t_s[px * 2 + py, s * C1 : (s + 1) * C1, :] = jnp.concatenate(rows, 0).T.astype(BF)

    buf_s[ROWS_ONE + ROWS_TWO :, :] = jnp.zeros((ROWS - ROWS_ONE - ROWS_TWO, C1), BF)
    for kx in range(3):
        px, dx = TAP[kx]
        for ky in range(3):
            py, dy = TAP[ky]
            d = nn(u2t_s[px * 2 + py], b_rows(dx, dy, CY)) * SCALE_TWO
            at = ROWS_ONE + (kx * 3 + ky) * 3 * C1
            buf_s[at : at + C1, :] = d[C1:, C2:].astype(BF)
            buf_s[at + C1 : at + 2 * C1, :] = d[0:C1, 0:C2].astype(BF)
            buf_s[at + 2 * C1 : at + 3 * C1, :] = d[C1:, 0:C2].astype(BF)

    for px in range(2):
        for py in range(2):
            for i in range(MX):
                for j in range(0, MY, 2):
                    pair = jnp.concatenate(
                        [u_ref[0, 2 * i + px, 2 * (j + e) + py] for e in range(2)], 0
                    )
                    at = (i * MY + j) * MZ
                    u1t_s[px * 2 + py, :, at : at + 2 * MZ] = pair.T

    for kx in range(3):
        px, dx = TAP[kx]
        for ky in range(3):
            py, dy = TAP[ky]
            total = None
            for i in range(MX):
                at = ((i + dx) * EY + dy) * MZ
                part = nn(
                    u1t_s[px * 2 + py, :, i * own : (i + 1) * own], a_ref[at : at + own, :]
                )
                total = part if total is None else total + part
            d = total * SCALE_ONE
            at = (kx * 3 + ky) * 3 * CIN
            buf_s[at : at + CIN, :] = d[CIN:, C1:].astype(BF)
            buf_s[at + CIN : at + 2 * CIN, :] = d[0:CIN, 0:C1].astype(BF)
            buf_s[at + 2 * CIN : at + 3 * CIN, :] = d[CIN:, 0:C1].astype(BF)

    core = core_ref[0]
    keep_ref[...] = buf_s[pl.ds(pl.multiple_of(core * HALF, HALF), HALF), :]
    send_ref[...] = buf_s[pl.ds(pl.multiple_of((1 - core) * HALF, HALF), HALF), :]


def input_kernel(a_ref, w1_ref, out_ref, r1_s):
    zero = jnp.zeros((CIN, C1), BF)
    for kx in range(3):
        for ky in range(3):
            at = SLOT[ky] * 2 * CIN
            r1_s[kx, at : at + CIN, 0:C1] = w1_ref[kx, ky, 1]
            r1_s[kx, at : at + CIN, C1:] = zero
            r1_s[kx, at + CIN : at + 2 * CIN, 0:C1] = w1_ref[kx, ky, 2]
            r1_s[kx, at + CIN : at + 2 * CIN, C1:] = w1_ref[kx, ky, 0]
    wide = 2 * CIN
    step = 4
    for i in range(MX):
        for px in range(2):
            for j in range(0, MY, step):
                both = None
                odd = None
                for kx, dx in TAPS[px]:
                    at = ((i + dx) * EY + j) * MZ
                    part = nt(a_ref[at : at + step * MZ, :], r1_s[kx, 0 : 2 * wide, :])
                    both = part if both is None else both + part
                    part = nt(a_ref[at + MZ : at + (step + 1) * MZ, :], r1_s[kx, 2 * wide :, :])
                    odd = part if odd is None else odd + part
                even = both[:, 0:wide].astype(BF)
                odd = (both[:, wide:] + odd).astype(BF)
                for e in range(step):
                    rows = slice(e * MZ, (e + 1) * MZ)
                    out_ref[0, 2 * i + px, 2 * (j + e)] = even[rows]
                    out_ref[0, 2 * i + px, 2 * (j + e) + 1] = odd[rows]


def vmem(n):
    return [pl.BlockSpec(memory_space=pltpu.VMEM)] * n


def main_call(core, u, pre, og, hx, hy, hc, w1, w2):
    return pl.pallas_call(
        main_kernel,
        out_shape=(
            jax.ShapeDtypeStruct((EX * EY * MZ, 2 * C1), BF),
            jax.ShapeDtypeStruct((HALF, C1), BF),
            jax.ShapeDtypeStruct((HALF, C1), BF),
        ),
        in_specs=[pl.BlockSpec(memory_space=pltpu.SMEM)] + vmem(8),
        out_specs=tuple(vmem(3)),
        scratch_shapes=[
            pltpu.VMEM((2 * (CY + 1) * CZ, 2 * C2), BF),
            pltpu.VMEM((9, 2 * C1, 2 * C2), BF),
            pltpu.VMEM((EX * EY * MZ, C1), F32),
            pltpu.VMEM((MX * MY * MZ, C1), F32),
            pltpu.VMEM((4, 2 * C1, CY * CZ), BF),
            pltpu.VMEM((4, 2 * CIN, MX * MY * MZ), BF),
            pltpu.VMEM((ROWS, C1), BF),
        ],
        cost_estimate=pl.CostEstimate(flops=2_000_000_000, bytes_accessed=8_000_000, transcendentals=0),
        name="main",
    )(core, u, pre, og, hx, hy, hc, w1, w2)


def input_call(a, w1):
    return pl.pallas_call(
        input_kernel,
        out_shape=jax.ShapeDtypeStruct((1, 2 * MX, 2 * MY, MZ, 2 * CIN), BF),
        in_specs=vmem(2),
        out_specs=vmem(1)[0],
        scratch_shapes=[pltpu.VMEM((3, 6 * CIN, 2 * C1), BF)],
        cost_estimate=pl.CostEstimate(flops=1_200_000_000, bytes_accessed=3_000_000, transcendentals=0),
        name="grad_input",
    )(a, w1)


def on_device(u, pre, og, w1, w2):
    core = lax.axis_index("core")
    sx = lax.axis_size("y") * lax.axis_size("xl")
    sz = lax.axis_size("zh") * lax.axis_size("zl")
    AX, AZ = ("y", "xl"), ("zh", "zl")
    from_x = [(i + 1, i) for i in range(sx - 1)]
    from_z = [(i + 1, i) for i in range(sz - 1)]
    from_xz = [
        ((i + 1) * sz + j + 1, i * sz + j) for i in range(sx - 1) for j in range(sz - 1)
    ]
    flat_pre = pre[0].reshape(MX, MY, MZ, C1)
    flat_og = og[0, 0]
    hx = jnp.concatenate([flat_og.reshape(-1, C2), flat_pre[0].reshape(-1, C1)], 0)
    hy = jnp.concatenate([flat_og[0], flat_pre[:, 0].reshape(-1, C1)], 0)
    hc = jnp.concatenate([flat_og[0], flat_pre[0, 0]], 0)
    hx = lax.ppermute(hx, AX, from_x)
    hy = lax.ppermute(hy, AZ, from_z)
    hc = lax.ppermute(hc, AX + AZ, from_xz)
    a, keep, send = main_call(core.reshape(1), u, pre, og, hx, hy, hc, w1, w2)
    received = lax.ppermute(send, "core", [(0, 1), (1, 0)])
    grad_input = input_call(a, w1)

    group = ("xh", "y", "xl", "zl")
    half = (keep.astype(F32) + received.astype(F32)).astype(BF).reshape(GROUP, CHUNK, C1)
    parts = lax.all_to_all(half, group, 0, 0, tiled=True)
    chunk = jnp.sum(parts.astype(F32), axis=0).astype(BF)
    parts = lax.all_to_all(jnp.broadcast_to(chunk[None], (4, CHUNK, C1)), "zh", 0, 0, tiled=True)
    chunk = jnp.sum(parts.astype(F32), axis=0).astype(BF)
    mine = lax.all_to_all(jnp.broadcast_to(chunk[None], (GROUP, CHUNK, C1)), group, 0, 0, tiled=True)
    mine = mine.reshape(HALF, C1)
    other = lax.ppermute(mine, "core", [(0, 1), (1, 0)])
    low = jnp.where(core == 0, mine, other).astype(F32)
    high = jnp.where(core == 0, other, mine).astype(F32)
    grad_one = low[:ROWS_ONE].reshape(3, 3, 3, CIN, C1)
    grad_two = jnp.concatenate([low[ROWS_ONE:], high[: ROWS_ONE + ROWS_TWO - HALF]], 0)
    return grad_input, grad_one, grad_two.reshape(3, 3, 3, C1, C2)


def solution(mesh):
    fine = Mesh(mesh.devices.reshape(2, 2, 4, 2, 4, 2), ("xh", "core", "y", "xl", "zh", "zl"))
    spec = P(("xh", "core"), ("y", "xl"), ("zh", "zl"), None, None)
    return jax.shard_map(
        on_device,
        mesh=fine,
        in_specs=(spec, spec, spec, P(), P()),
        out_specs=(spec, P(), P()),
        check_vma=False,
    )
```

```python
import functools

import jax
import jax.numpy as jnp
from jax import lax
from jax.experimental import pallas as pl
from jax.experimental.pallas import tpu as pltpu
from jax.sharding import Mesh
from jax.sharding import PartitionSpec as P

BF = jnp.bfloat16
F32 = jnp.float32

CX, CY, CZ = 1, 4, 32
MX, MY, MZ = 2, 8, 64
CIN, C1, C2 = 64, 128, 128
EX, EY = MX + 1, MY + 1
CHUNK = 88
GROUP = 32
HALF = CHUNK * GROUP
ROWS_ONE = 27 * CIN
ROWS_TWO = 27 * C1
ROWS = 2 * HALF
SCALE_ONE = float(4 * 16 * 64 * 64) ** (-0.5)
SCALE_TWO = float(4 * 8 * 32 * 32) ** (-0.5)

TAP = ((1, 1), (0, 0), (1, 0))
TAPS = (((1, 0),), ((2, 0), (0, 1)))
SLOT = (2, 0, 1)


def nt(a, b):
    return lax.dot_general(a, b, (((1,), (1,)), ((), ())), preferred_element_type=F32)


def nn(a, b):
    return lax.dot_general(a, b, (((1,), (0,)), ((), ())), preferred_element_type=F32)


def next_row(value, period):
    rows = value.shape[0]
    rolled = pltpu.roll(value, rows - 1, 0)
    row = lax.broadcasted_iota(jnp.int32, value.shape, 0)
    return jnp.where(row % period == period - 1, 0.0, rolled)


def pack_kernel(pre_ref, og_ref, hx_ref, hy_ref, hc_ref, sems):
    copies = []

    def copy(src, dst):
        copies.append(pltpu.make_async_copy(src, dst, sems.at[len(copies)]))
        copies[-1].start()

    for j in range(CY):
        copy(og_ref.at[0, 0, j], hx_ref.at[pl.ds(j * CZ, CZ)])
    for y in range(MY):
        copy(pre_ref.at[0, 0, y], hx_ref.at[pl.ds(CY * CZ + y * MZ, MZ)])
    copy(og_ref.at[0, 0, 0], hy_ref.at[pl.ds(0, CZ)])
    for x in range(MX):
        copy(pre_ref.at[0, x, 0], hy_ref.at[pl.ds(CZ + x * MZ, MZ)])
    copy(og_ref.at[0, 0, 0], hc_ref.at[pl.ds(0, CZ)])
    copy(pre_ref.at[0, 0, 0], hc_ref.at[pl.ds(CZ, MZ)])
    for c in copies:
        c.wait()


def prep_kernel(u_ref, pre_ref, w1_ref, w2_ref, r1_ref, r2_ref, u1t_ref, u2t_ref, act_s):
    zero = jnp.zeros((CIN, C1), BF)
    for kx in range(3):
        for ky in range(3):
            at = SLOT[ky] * 2 * CIN
            r1_ref[kx, at : at + CIN, 0:C1] = w1_ref[kx, ky, 1]
            r1_ref[kx, at : at + CIN, C1:] = zero
            r1_ref[kx, at + CIN : at + 2 * CIN, 0:C1] = w1_ref[kx, ky, 2]
            r1_ref[kx, at + CIN : at + 2 * CIN, C1:] = w1_ref[kx, ky, 0]

    zero = jnp.zeros((C1, C2), BF)
    for kx in range(3):
        for ky in range(3):
            t = kx * 3 + ky
            r2_ref[t, 0:C1, 0:C2] = w2_ref[kx, ky, 1]
            r2_ref[t, 0:C1, C2:] = zero
            r2_ref[t, C1:, 0:C2] = w2_ref[kx, ky, 2]
            r2_ref[t, C1:, C2:] = w2_ref[kx, ky, 0]

    own = MY * MZ
    for mx in range(MX):
        pre = pre_ref[0, mx].reshape(own, C1).astype(F32)
        act_s[mx * own : (mx + 1) * own, :] = jnp.where(pre > 0, pre, 0.3 * pre)
    for px in range(2):
        for py in range(2):
            for s in range(2):
                rows = [
                    act_s[pl.ds((px * MY + 2 * j + py) * MZ + s, CZ, stride=2), :]
                    for j in range(CY)
                ]
                u2t_ref[px * 2 + py, s * C1 : (s + 1) * C1, :] = jnp.concatenate(rows, 0).T.astype(BF)

    for px in range(2):
        for py in range(2):
            for i in range(MX):
                for j in range(0, MY, 2):
                    pair = jnp.concatenate(
                        [u_ref[0, 2 * i + px, 2 * (j + e) + py] for e in range(2)], 0
                    )
                    at = (i * MY + j) * MZ
                    u1t_ref[px * 2 + py, :, at : at + 2 * MZ] = pair.T


def main_kernel(
    core_ref, pre_ref, og_ref, hx_ref, hy_ref, hc_ref, r2_ref, u1t_ref, u2t_ref,
    a_ref, keep_ref, send_ref,
    b_s, ga_s, buf_s,
):
    def put_b(at, value):
        n = value.shape[0]
        b_s[at : at + n, 0:C2] = value
        b_s[at : at + n, C2:] = next_row(value.astype(F32), CZ).astype(BF)

    put_b(0, og_ref[0, 0].reshape(CY * CZ, C2))
    put_b(CY * CZ, hy_ref[0:CZ])
    put_b((CY + 1) * CZ, hx_ref[0 : CY * CZ])
    put_b((2 * CY + 1) * CZ, hc_ref[0:CZ])

    def put_ga(mx, my, value):
        base = (mx * EY + my) * MZ
        ga_s[pl.ds(base, CZ, stride=2), :] = value[:, 0:C1]
        ga_s[pl.ds(base + 1, CZ, stride=2), :] = value[:, C1:]

    def b_rows(i, j, n):
        at = (i * (CY + 1) + j) * CZ
        return b_s[at : at + n * CZ, :]

    for px in range(2):
        for i in range(2 - px):
            for py in range(2):
                n = CY + 1 - py
                total = None
                for kx, dx in TAPS[px]:
                    for ky, dy in TAPS[py]:
                        part = nt(b_rows(i + dx, dy, n), r2_ref[kx * 3 + ky])
                        total = part if total is None else total + part
                for j in range(n):
                    put_ga(2 * i + px, 2 * j + py, total[j * CZ : (j + 1) * CZ])

    def put_a(at, pre):
        n = pre.shape[0]
        slope = jnp.where(pre.astype(F32) > 0, 1.0, 0.3)
        value = ga_s[at : at + n, :] * slope
        a_ref[at : at + n, 0:C1] = value.astype(BF)
        a_ref[at : at + n, C1:] = next_row(value, MZ).astype(BF)

    own = MY * MZ
    for mx in range(MX):
        put_a(mx * EY * MZ, pre_ref[0, mx].reshape(own, C1))
        put_a((mx * EY + MY) * MZ, hy_ref[CZ + mx * MZ : CZ + (mx + 1) * MZ])
    put_a(MX * EY * MZ, hx_ref[CY * CZ : CY * CZ + own])
    put_a((MX * EY + MY) * MZ, hc_ref[CZ : CZ + MZ])

    buf_s[ROWS_ONE + ROWS_TWO :, :] = jnp.zeros((ROWS - ROWS_ONE - ROWS_TWO, C1), BF)
    for kx in range(3):
        px, dx = TAP[kx]
        for ky in range(3):
            py, dy = TAP[ky]
            d = nn(u2t_ref[px * 2 + py], b_rows(dx, dy, CY)) * SCALE_TWO
            at = ROWS_ONE + (kx * 3 + ky) * 3 * C1
            buf_s[at : at + C1, :] = d[C1:, C2:].astype(BF)
            buf_s[at + C1 : at + 2 * C1, :] = d[0:C1, 0:C2].astype(BF)
            buf_s[at + 2 * C1 : at + 3 * C1, :] = d[C1:, 0:C2].astype(BF)

    for kx in range(3):
        px, dx = TAP[kx]
        for ky in range(3):
            py, dy = TAP[ky]
            total = None
            for i in range(MX):
                at = ((i + dx) * EY + dy) * MZ
                part = nn(
                    u1t_ref[px * 2 + py, :, i * own : (i + 1) * own], a_ref[at : at + own, :]
                )
                total = part if total is None else total + part
            d = total * SCALE_ONE
            at = (kx * 3 + ky) * 3 * CIN
            buf_s[at : at + CIN, :] = d[CIN:, C1:].astype(BF)
            buf_s[at + CIN : at + 2 * CIN, :] = d[0:CIN, 0:C1].astype(BF)
            buf_s[at + 2 * CIN : at + 3 * CIN, :] = d[CIN:, 0:C1].astype(BF)

    core = core_ref[0]
    keep_ref[...] = buf_s[pl.ds(pl.multiple_of(core * HALF, HALF), HALF), :]
    send_ref[...] = buf_s[pl.ds(pl.multiple_of((1 - core) * HALF, HALF), HALF), :]


def input_kernel(a_ref, r1_ref, out_ref):
    wide = 2 * CIN
    step = 4
    for i in range(MX):
        for px in range(2):
            for j in range(0, MY, step):
                both = None
                odd = None
                for kx, dx in TAPS[px]:
                    at = ((i + dx) * EY + j) * MZ
                    part = nt(a_ref[at : at + step * MZ, :], r1_ref[kx, 0 : 2 * wide, :])
                    both = part if both is None else both + part
                    part = nt(a_ref[at + MZ : at + (step + 1) * MZ, :], r1_ref[kx, 2 * wide :, :])
                    odd = part if odd is None else odd + part
                even = both[:, 0:wide].astype(BF)
                odd = (both[:, wide:] + odd).astype(BF)
                for e in range(step):
                    rows = slice(e * MZ, (e + 1) * MZ)
                    out_ref[0, 2 * i + px, 2 * (j + e)] = even[rows]
                    out_ref[0, 2 * i + px, 2 * (j + e) + 1] = odd[rows]


def output_kernel(core_ref, mine_ref, other_ref, one_ref, two_ref):
    low = HALF - ROWS_ONE
    high = ROWS_TWO - low

    def put(first_ref, second_ref):
        one_ref[...] = first_ref[0:ROWS_ONE].astype(F32)
        two_ref[0:low] = first_ref[ROWS_ONE:].astype(F32)
        two_ref[low:] = second_ref[0:high].astype(F32)

    @pl.when(core_ref[0] == 0)
    def _():
        put(mine_ref, other_ref)

    @pl.when(core_ref[0] != 0)
    def _():
        put(other_ref, mine_ref)


def vmem(n):
    return [pl.BlockSpec(memory_space=pltpu.VMEM)] * n


def near(x):
    return pltpu.with_memory_space_constraint(x, pltpu.VMEM)


SMEM = pl.BlockSpec(memory_space=pltpu.SMEM)
LIMIT = 20 * 1024 * 1024


def call(kernel, name, out, scratch, in_specs, flops, bytes_moved):
    return pl.pallas_call(
        kernel,
        out_shape=tuple(out),
        in_specs=in_specs,
        out_specs=tuple(vmem(len(out))),
        scratch_shapes=scratch,
        cost_estimate=pl.CostEstimate(flops=flops, bytes_accessed=bytes_moved, transcendentals=0),
        compiler_params=pltpu.CompilerParams(vmem_limit_bytes=LIMIT),
        name=name,
    )


def pack_call(pre, og):
    out = [pltpu.VMEM(((CY * CZ + MY * MZ), C1), BF), pltpu.VMEM((CZ + MX * MZ, C1), BF), pltpu.VMEM((CZ + MZ, C1), BF)]
    count = CY + MY + 1 + MX + 2
    any_spec = [pl.BlockSpec(memory_space=pl.ANY)] * 2
    return call(pack_kernel, "pack", out, [pltpu.SemaphoreType.DMA((count,))], any_spec, 0, 500_000)(pre, og)


def prep_call(u, pre, w1, w2):
    out = [
        pltpu.VMEM((3, 6 * CIN, 2 * C1), BF),
        pltpu.VMEM((9, 2 * C1, 2 * C2), BF),
        pltpu.VMEM((4, 2 * CIN, MX * MY * MZ), BF),
        pltpu.VMEM((4, 2 * C1, CY * CZ), BF),
    ]
    scratch = [pltpu.VMEM((MX * MY * MZ, C1), F32)]
    return call(prep_kernel, "prep", out, scratch, vmem(4), 0, 6_000_000)(u, pre, w1, w2)


def main_call(core, pre, og, hx, hy, hc, r2, u1t, u2t):
    out = [
        pltpu.VMEM((EX * EY * MZ, 2 * C1), BF),
        pltpu.VMEM((HALF, C1), BF),
        pltpu.VMEM((HALF, C1), BF),
    ]
    scratch = [
        pltpu.VMEM((2 * (CY + 1) * CZ, 2 * C2), BF),
        pltpu.VMEM((EX * EY * MZ, C1), F32),
        pltpu.VMEM((ROWS, C1), BF),
    ]
    return call(main_kernel, "main", out, scratch, [SMEM] + vmem(8), 2_000_000_000, 8_000_000)(
        core, pre, og, hx, hy, hc, r2, u1t, u2t
    )


def input_call(a, r1):
    out = [jax.ShapeDtypeStruct((1, 2 * MX, 2 * MY, MZ, 2 * CIN), BF)]
    return call(input_kernel, "grad_input", out, [], vmem(2), 1_200_000_000, 3_000_000)(a, r1)[0]


def output_call(core, mine, other):
    out = [jax.ShapeDtypeStruct((ROWS_ONE, C1), F32), jax.ShapeDtypeStruct((ROWS_TWO, C1), F32)]
    return call(output_kernel, "output", out, [], [SMEM] + vmem(2), 0, 4_000_000)(core, mine, other)


def on_device(u, pre, og, w1, w2):
    core = lax.axis_index("core").reshape(1)
    sx = lax.axis_size("y") * lax.axis_size("xl")
    sz = lax.axis_size("zh") * lax.axis_size("zl")
    AX, AZ = ("y", "xl"), ("zh", "zl")
    from_x = [(i + 1, i) for i in range(sx - 1)]
    from_z = [(i + 1, i) for i in range(sz - 1)]
    from_xz = [
        ((i + 1) * sz + j + 1, i * sz + j) for i in range(sx - 1) for j in range(sz - 1)
    ]
    hx, hy, hc = pack_call(pre, og)
    hx = lax.ppermute(hx, AX, from_x)
    hc = lax.ppermute(hc, AX + AZ, from_xz)
    hy = lax.ppermute(hy, AZ, from_z)
    r1, r2, u1t, u2t = prep_call(u, pre, w1, w2)
    a, keep, send = main_call(core, pre, og, hx, hy, hc, r2, u1t, u2t)
    received = lax.ppermute(send, "core", [(0, 1), (1, 0)])
    grad_input = input_call(a, r1)

    group = ("xh", "y", "xl", "zl")
    half = (keep.astype(F32) + received.astype(F32)).astype(BF).reshape(GROUP, CHUNK, C1)
    parts = lax.all_to_all(half, group, 0, 0, tiled=True)
    chunk = jnp.sum(parts.astype(F32), axis=0).astype(BF)
    parts = lax.all_to_all(jnp.broadcast_to(chunk[None], (4, CHUNK, C1)), "zh", 0, 0, tiled=True)
    chunk = jnp.sum(parts.astype(F32), axis=0).astype(BF)
    mine = lax.all_to_all(jnp.broadcast_to(chunk[None], (GROUP, CHUNK, C1)), group, 0, 0, tiled=True)
    mine = mine.reshape(HALF, C1)
    other = lax.ppermute(mine, "core", [(0, 1), (1, 0)])
    grad_one, grad_two = output_call(core, mine, other)
    return grad_input, grad_one.reshape(3, 3, 3, CIN, C1), grad_two.reshape(3, 3, 3, C1, C2)


def solution(mesh):
    fine = Mesh(mesh.devices.reshape(2, 2, 4, 2, 4, 2), ("xh", "core", "y", "xl", "zh", "zl"))
    spec = P(("xh", "core"), ("y", "xl"), ("zh", "zl"), None, None)
    return jax.shard_map(
        on_device,
        mesh=fine,
        in_specs=(spec, spec, spec, P(), P()),
        out_specs=(spec, P(), P()),
        check_vma=False,
    )
```

```python
import functools

import jax
import jax.numpy as jnp
from jax import lax
from jax.experimental import pallas as pl
from jax.experimental.pallas import tpu as pltpu
from jax.sharding import Mesh
from jax.sharding import PartitionSpec as P

BF = jnp.bfloat16
F32 = jnp.float32

CX, CY, CZ = 1, 4, 32
MX, MY, MZ = 2, 8, 64
CIN, C1, C2 = 64, 128, 128
EX, EY = MX + 1, MY + 1
CHUNK = 88
GROUP = 32
HALF = CHUNK * GROUP
ROWS_ONE = 27 * CIN
ROWS_TWO = 27 * C1
ROWS = 2 * HALF
SCALE_ONE = float(4 * 16 * 64 * 64) ** (-0.5)
SCALE_TWO = float(4 * 8 * 32 * 32) ** (-0.5)

TAP = ((1, 1), (0, 0), (1, 0))
TAPS = (((1, 0),), ((2, 0), (0, 1)))
SLOT = (2, 0, 1)


def nt(a, b):
    return lax.dot_general(a, b, (((1,), (1,)), ((), ())), preferred_element_type=F32)


def nn(a, b):
    return lax.dot_general(a, b, (((1,), (0,)), ((), ())), preferred_element_type=F32)


def next_row(value, period):
    rows = value.shape[0]
    rolled = pltpu.roll(value, rows - 1, 0)
    row = lax.broadcasted_iota(jnp.int32, value.shape, 0)
    return jnp.where(row % period == period - 1, 0.0, rolled)


def pack_kernel(pre_ref, og_ref, hx_ref, hy_ref, hc_ref, sems):
    copies = []

    def copy(src, dst):
        copies.append(pltpu.make_async_copy(src, dst, sems.at[len(copies)]))
        copies[-1].start()

    for j in range(CY):
        copy(og_ref.at[0, 0, j], hx_ref.at[pl.ds(j * CZ, CZ)])
    for y in range(MY):
        copy(pre_ref.at[0, 0, y], hx_ref.at[pl.ds(CY * CZ + y * MZ, MZ)])
    copy(og_ref.at[0, 0, 0], hy_ref.at[pl.ds(0, CZ)])
    for x in range(MX):
        copy(pre_ref.at[0, x, 0], hy_ref.at[pl.ds(CZ + x * MZ, MZ)])
    copy(og_ref.at[0, 0, 0], hc_ref.at[pl.ds(0, CZ)])
    copy(pre_ref.at[0, 0, 0], hc_ref.at[pl.ds(CZ, MZ)])
    for c in copies:
        c.wait()


def prep_kernel(
    u_hbm, pre_hbm, og_hbm, w1_hbm, w2_hbm,
    r1_ref, r2_ref, u1t_ref, u2t_ref, pre_ref, og_ref,
    u_ref, w1_ref, w2_ref, act_s, sems,
):
    w1_copy, w2_copy, pre_copy, u_copy, og_copy = [
        pltpu.make_async_copy(source, target, sems.at[k])
        for k, (source, target) in enumerate(
            ((w1_hbm, w1_ref), (w2_hbm, w2_ref), (pre_hbm, pre_ref), (u_hbm, u_ref), (og_hbm, og_ref))
        )
    ]
    for copy in (w1_copy, w2_copy, pre_copy, u_copy, og_copy):
        copy.start()
    w1_copy.wait()
    zero = jnp.zeros((CIN, C1), BF)
    for kx in range(3):
        for ky in range(3):
            at = SLOT[ky] * 2 * CIN
            r1_ref[kx, at : at + CIN, 0:C1] = w1_ref[kx, ky, 1]
            r1_ref[kx, at : at + CIN, C1:] = zero
            r1_ref[kx, at + CIN : at + 2 * CIN, 0:C1] = w1_ref[kx, ky, 2]
            r1_ref[kx, at + CIN : at + 2 * CIN, C1:] = w1_ref[kx, ky, 0]

    w2_copy.wait()
    zero = jnp.zeros((C1, C2), BF)
    for kx in range(3):
        for ky in range(3):
            t = kx * 3 + ky
            r2_ref[t, 0:C1, 0:C2] = w2_ref[kx, ky, 1]
            r2_ref[t, 0:C1, C2:] = zero
            r2_ref[t, C1:, 0:C2] = w2_ref[kx, ky, 2]
            r2_ref[t, C1:, C2:] = w2_ref[kx, ky, 0]

    pre_copy.wait()
    own = MY * MZ
    for mx in range(MX):
        pre = pre_ref[0, mx].reshape(own, C1).astype(F32)
        act_s[mx * own : (mx + 1) * own, :] = jnp.where(pre > 0, pre, 0.3 * pre)
    for px in range(2):
        for py in range(2):
            for s in range(2):
                rows = [
                    act_s[pl.ds((px * MY + 2 * j + py) * MZ + s, CZ, stride=2), :]
                    for j in range(CY)
                ]
                u2t_ref[px * 2 + py, s * C1 : (s + 1) * C1, :] = jnp.concatenate(rows, 0).T.astype(BF)

    u_copy.wait()
    for px in range(2):
        for py in range(2):
            for i in range(MX):
                for j in range(0, MY, 2):
                    pair = jnp.concatenate(
                        [u_ref[0, 2 * i + px, 2 * (j + e) + py] for e in range(2)], 0
                    )
                    at = (i * MY + j) * MZ
                    u1t_ref[px * 2 + py, :, at : at + 2 * MZ] = pair.T
    og_copy.wait()


def main_kernel(
    core_ref, pre_ref, og_ref, hx_ref, hy_ref, hc_ref, r2_ref, u1t_ref, u2t_ref,
    a_ref, keep_ref, send_ref,
    b_s, ga_s, buf_s,
):
    def put_b(at, value):
        n = value.shape[0]
        b_s[at : at + n, 0:C2] = value
        b_s[at : at + n, C2:] = next_row(value.astype(F32), CZ).astype(BF)

    put_b(0, og_ref[0, 0].reshape(CY * CZ, C2))
    put_b(CY * CZ, hy_ref[0:CZ])
    put_b((CY + 1) * CZ, hx_ref[0 : CY * CZ])
    put_b((2 * CY + 1) * CZ, hc_ref[0:CZ])

    def put_ga(mx, my, value):
        base = (mx * EY + my) * MZ
        ga_s[pl.ds(base, CZ, stride=2), :] = value[:, 0:C1]
        ga_s[pl.ds(base + 1, CZ, stride=2), :] = value[:, C1:]

    def b_rows(i, j, n):
        at = (i * (CY + 1) + j) * CZ
        return b_s[at : at + n * CZ, :]

    for px in range(2):
        for i in range(2 - px):
            for py in range(2):
                n = CY + 1 - py
                total = None
                for kx, dx in TAPS[px]:
                    for ky, dy in TAPS[py]:
                        part = nt(b_rows(i + dx, dy, n), r2_ref[kx * 3 + ky])
                        total = part if total is None else total + part
                for j in range(n):
                    put_ga(2 * i + px, 2 * j + py, total[j * CZ : (j + 1) * CZ])

    def put_a(at, pre):
        n = pre.shape[0]
        slope = jnp.where(pre.astype(F32) > 0, 1.0, 0.3)
        value = ga_s[at : at + n, :] * slope
        a_ref[at : at + n, 0:C1] = value.astype(BF)
        a_ref[at : at + n, C1:] = next_row(value, MZ).astype(BF)

    own = MY * MZ
    for mx in range(MX):
        put_a(mx * EY * MZ, pre_ref[0, mx].reshape(own, C1))
        put_a((mx * EY + MY) * MZ, hy_ref[CZ + mx * MZ : CZ + (mx + 1) * MZ])
    put_a(MX * EY * MZ, hx_ref[CY * CZ : CY * CZ + own])
    put_a((MX * EY + MY) * MZ, hc_ref[CZ : CZ + MZ])

    buf_s[ROWS_ONE + ROWS_TWO :, :] = jnp.zeros((ROWS - ROWS_ONE - ROWS_TWO, C1), BF)
    for kx in range(3):
        px, dx = TAP[kx]
        for ky in range(3):
            py, dy = TAP[ky]
            d = nn(u2t_ref[px * 2 + py], b_rows(dx, dy, CY)) * SCALE_TWO
            at = ROWS_ONE + (kx * 3 + ky) * 3 * C1
            buf_s[at : at + C1, :] = d[C1:, C2:].astype(BF)
            buf_s[at + C1 : at + 2 * C1, :] = d[0:C1, 0:C2].astype(BF)
            buf_s[at + 2 * C1 : at + 3 * C1, :] = d[C1:, 0:C2].astype(BF)

    for kx in range(3):
        px, dx = TAP[kx]
        for ky in range(3):
            py, dy = TAP[ky]
            total = None
            for i in range(MX):
                at = ((i + dx) * EY + dy) * MZ
                part = nn(
                    u1t_ref[px * 2 + py, :, i * own : (i + 1) * own], a_ref[at : at + own, :]
                )
                total = part if total is None else total + part
            d = total * SCALE_ONE
            at = (kx * 3 + ky) * 3 * CIN
            buf_s[at : at + CIN, :] = d[CIN:, C1:].astype(BF)
            buf_s[at + CIN : at + 2 * CIN, :] = d[0:CIN, 0:C1].astype(BF)
            buf_s[at + 2 * CIN : at + 3 * CIN, :] = d[CIN:, 0:C1].astype(BF)

    core = core_ref[0]
    keep_ref[...] = buf_s[pl.ds(pl.multiple_of(core * HALF, HALF), HALF), :]
    send_ref[...] = buf_s[pl.ds(pl.multiple_of((1 - core) * HALF, HALF), HALF), :]


def input_kernel(a_ref, r1_ref, out_ref):
    wide = 2 * CIN
    step = 4
    for i in range(MX):
        for px in range(2):
            for j in range(0, MY, step):
                both = None
                odd = None
                for kx, dx in TAPS[px]:
                    at = ((i + dx) * EY + j) * MZ
                    part = nt(a_ref[at : at + step * MZ, :], r1_ref[kx, 0 : 2 * wide, :])
                    both = part if both is None else both + part
                    part = nt(a_ref[at + MZ : at + (step + 1) * MZ, :], r1_ref[kx, 2 * wide :, :])
                    odd = part if odd is None else odd + part
                even = both[:, 0:wide].astype(BF)
                odd = (both[:, wide:] + odd).astype(BF)
                for e in range(step):
                    rows = slice(e * MZ, (e + 1) * MZ)
                    out_ref[0, 2 * i + px, 2 * (j + e)] = even[rows]
                    out_ref[0, 2 * i + px, 2 * (j + e) + 1] = odd[rows]


def output_kernel(second, core_ref, half_ref, *refs):
    one_hbm, two_hbm, wide, sems = refs[-4:]
    low = HALF - ROWS_ONE
    high = ROWS_TWO - low

    def put(parts):
        copies = []
        for k, (at, rows, target, to) in enumerate(parts):
            wide[at : at + rows] = half_ref[at : at + rows].astype(F32)
            copies.append(
                pltpu.make_async_copy(
                    wide.at[pl.ds(at, rows)], target.at[pl.ds(to, rows)], sems.at[k]
                )
            )
            copies[-1].start()
        for copy in copies:
            copy.wait()

    @pl.when(core_ref[0] == second)
    def _():
        put(((0, ROWS_ONE // 2, one_hbm, 0), (ROWS_ONE // 2, ROWS_ONE // 2, one_hbm, ROWS_ONE // 2), (ROWS_ONE, low, two_hbm, 0)))

    @pl.when(core_ref[0] != second)
    def _():
        third = 792
        put(((0, third, two_hbm, low), (third, third, two_hbm, low + third), (2 * third, high - 2 * third, two_hbm, low + 2 * third)))


def vmem(n):
    return [pl.BlockSpec(memory_space=pltpu.VMEM)] * n


def hbm(n):
    return [pl.BlockSpec(memory_space=pltpu.HBM)] * n


def far(*arrays):
    return [pltpu.with_memory_space_constraint(x, pltpu.HBM) for x in arrays]


SMEM = pl.BlockSpec(memory_space=pltpu.SMEM)
LIMIT = 20 * 1024 * 1024


def call(kernel, name, out, scratch, in_specs, flops, bytes_moved):
    return pl.pallas_call(
        kernel,
        out_shape=tuple(out),
        in_specs=in_specs,
        out_specs=tuple(vmem(len(out))),
        scratch_shapes=scratch,
        cost_estimate=pl.CostEstimate(flops=flops, bytes_accessed=bytes_moved, transcendentals=0),
        compiler_params=pltpu.CompilerParams(vmem_limit_bytes=LIMIT),
        name=name,
    )


def pack_call(pre, og):
    out = [pltpu.VMEM(((CY * CZ + MY * MZ), C1), BF), pltpu.VMEM((CZ + MX * MZ, C1), BF), pltpu.VMEM((CZ + MZ, C1), BF)]
    count = CY + MY + 1 + MX + 2
    return call(pack_kernel, "pack", out, [pltpu.SemaphoreType.DMA((count,))], hbm(2), 0, 500_000)(*far(pre, og))


def prep_call(u, pre, og, w1, w2):
    out = [
        pltpu.VMEM((3, 6 * CIN, 2 * C1), BF),
        pltpu.VMEM((9, 2 * C1, 2 * C2), BF),
        pltpu.VMEM((4, 2 * CIN, MX * MY * MZ), BF),
        pltpu.VMEM((4, 2 * C1, CY * CZ), BF),
        pltpu.VMEM(pre.shape, BF),
        pltpu.VMEM(og.shape, BF),
    ]
    scratch = [
        pltpu.VMEM(u.shape, BF),
        pltpu.VMEM(w1.shape, BF),
        pltpu.VMEM(w2.shape, BF),
        pltpu.VMEM((MX * MY * MZ, C1), F32),
        pltpu.SemaphoreType.DMA((5,)),
    ]
    return call(prep_kernel, "prep", out, scratch, hbm(5), 0, 6_000_000)(*far(u, pre, og, w1, w2))


def main_call(core, pre, og, hx, hy, hc, r2, u1t, u2t):
    out = [
        pltpu.VMEM((EX * EY * MZ, 2 * C1), BF),
        pltpu.VMEM((HALF, C1), BF),
        pltpu.VMEM((HALF, C1), BF),
    ]
    scratch = [
        pltpu.VMEM((2 * (CY + 1) * CZ, 2 * C2), BF),
        pltpu.VMEM((EX * EY * MZ, C1), F32),
        pltpu.VMEM((ROWS, C1), BF),
    ]
    return call(main_kernel, "main", out, scratch, [SMEM] + vmem(8), 2_000_000_000, 8_000_000)(
        core, pre, og, hx, hy, hc, r2, u1t, u2t
    )


def input_call(a, r1):
    out = [jax.ShapeDtypeStruct((1, 2 * MX, 2 * MY, MZ, 2 * CIN), BF)]
    return call(input_kernel, "grad_input", out, [], vmem(2), 1_200_000_000, 3_000_000)(a, r1)[0]


def output_call(core, half, before=()):
    second = len(before) // 2
    return pl.pallas_call(
        functools.partial(output_kernel, second),
        out_shape=(
            jax.ShapeDtypeStruct((ROWS_ONE, C1), F32),
            jax.ShapeDtypeStruct((ROWS_TWO, C1), F32),
        ),
        in_specs=[SMEM] + vmem(1) + hbm(len(before)),
        out_specs=tuple(hbm(2)),
        scratch_shapes=[pltpu.VMEM((HALF, C1), F32), pltpu.SemaphoreType.DMA((3,))],
        input_output_aliases={2: 0, 3: 1} if second else {},
        cost_estimate=pl.CostEstimate(flops=0, bytes_accessed=2_000_000, transcendentals=0),
        compiler_params=pltpu.CompilerParams(vmem_limit_bytes=LIMIT),
        name="output",
    )(core, half, *before)


def on_device(u, pre, og, w1, w2):
    core = lax.axis_index("core").reshape(1)
    sx = lax.axis_size("y") * lax.axis_size("xl")
    sz = lax.axis_size("zh") * lax.axis_size("zl")
    AX, AZ = ("y", "xl"), ("zh", "zl")
    from_x = [(i + 1, i) for i in range(sx - 1)]
    from_z = [(i + 1, i) for i in range(sz - 1)]
    from_xz = [
        ((i + 1) * sz + j + 1, i * sz + j) for i in range(sx - 1) for j in range(sz - 1)
    ]
    hx, hy, hc = pack_call(pre, og)
    hx = lax.ppermute(hx, AX, from_x)
    hc = lax.ppermute(hc, AX + AZ, from_xz)
    hy = lax.ppermute(hy, AZ, from_z)
    r1, r2, u1t, u2t, pre, og = prep_call(u, pre, og, w1, w2)
    a, keep, send = main_call(core, pre, og, hx, hy, hc, r2, u1t, u2t)
    received = lax.ppermute(send, "core", [(0, 1), (1, 0)])
    grad_input = input_call(a, r1)
    received, grad_input = lax.optimization_barrier((received, grad_input))

    group = ("xh", "y", "xl", "zl")
    half = (keep.astype(F32) + received.astype(F32)).astype(BF).reshape(GROUP, CHUNK, C1)
    parts = lax.all_to_all(half, group, 0, 0, tiled=True)
    chunk = jnp.sum(parts.astype(F32), axis=0).astype(BF)
    parts = lax.all_to_all(jnp.broadcast_to(chunk[None], (4, CHUNK, C1)), "zh", 0, 0, tiled=True)
    chunk = jnp.sum(parts.astype(F32), axis=0).astype(BF)
    mine = lax.all_to_all(jnp.broadcast_to(chunk[None], (GROUP, CHUNK, C1)), group, 0, 0, tiled=True)
    mine = mine.reshape(HALF, C1)
    other = lax.ppermute(mine, "core", [(0, 1), (1, 0)])
    grad_one, grad_two = output_call(core, other, output_call(core, mine))
    return grad_input, grad_one.reshape(3, 3, 3, CIN, C1), grad_two.reshape(3, 3, 3, C1, C2)


def solution(mesh):
    fine = Mesh(mesh.devices.reshape(2, 2, 4, 2, 4, 2), ("xh", "core", "y", "xl", "zh", "zl"))
    spec = P(("xh", "core"), ("y", "xl"), ("zh", "zl"), None, None)
    return jax.shard_map(
        on_device,
        mesh=fine,
        in_specs=(spec, spec, spec, P(), P()),
        out_specs=(spec, P(), P()),
        check_vma=False,
    )
```

```python
import functools

import jax
import jax.numpy as jnp
from jax import lax
from jax.experimental import pallas as pl
from jax.experimental.pallas import tpu as pltpu
from jax.sharding import Mesh
from jax.sharding import PartitionSpec as P

BF = jnp.bfloat16
F32 = jnp.float32

CX, CY, CZ = 1, 4, 32
MX, MY, MZ = 2, 8, 64
CIN, C1, C2 = 64, 128, 128
EX, EY = MX + 1, MY + 1
CHUNK = 88
AX = ("y", "xl")
AZ = ("zh", "zl")
GROUP = 32
HALF = CHUNK * GROUP
ROWS_ONE = 27 * CIN
ROWS_TWO = 27 * C1
ROWS = 2 * HALF
SCALE_ONE = float(4 * 16 * 64 * 64) ** (-0.5)
SCALE_TWO = float(4 * 8 * 32 * 32) ** (-0.5)

TAP = ((1, 1), (0, 0), (1, 0))
TAPS = (((1, 0),), ((2, 0), (0, 1)))
SLOT = (2, 0, 1)


def nt(a, b):
    return lax.dot_general(a, b, (((1,), (1,)), ((), ())), preferred_element_type=F32)


def nn(a, b):
    return lax.dot_general(a, b, (((1,), (0,)), ((), ())), preferred_element_type=F32)


def next_row(value, period):
    rows = value.shape[0]
    rolled = pltpu.roll(value, rows - 1, 0)
    row = lax.broadcasted_iota(jnp.int32, value.shape, 0)
    return jnp.where(row % period == period - 1, 0.0, rolled)


def pack_kernel(pre_ref, og_ref, hx_ref, hy_ref, hc_ref, sems):
    copies = []

    def copy(src, dst):
        copies.append(pltpu.make_async_copy(src, dst, sems.at[len(copies)]))
        copies[-1].start()

    for j in range(CY):
        copy(og_ref.at[0, 0, j], hx_ref.at[pl.ds(j * CZ, CZ)])
    for y in range(MY):
        copy(pre_ref.at[0, 0, y], hx_ref.at[pl.ds(CY * CZ + y * MZ, MZ)])
    copy(og_ref.at[0, 0, 0], hy_ref.at[pl.ds(0, CZ)])
    for x in range(MX):
        copy(pre_ref.at[0, x, 0], hy_ref.at[pl.ds(CZ + x * MZ, MZ)])
    copy(og_ref.at[0, 0, 0], hc_ref.at[pl.ds(0, CZ)])
    copy(pre_ref.at[0, 0, 0], hc_ref.at[pl.ds(CZ, MZ)])
    for c in copies:
        c.wait()


def prep_kernel(
    u_hbm, pre_hbm, og_hbm, w1_hbm, w2_hbm,
    r1_ref, r2_ref, u1t_ref, u2t_ref, pre_ref, og_ref,
    u_ref, w1_ref, w2_ref, act_s, sems,
):
    w1_copy, w2_copy, pre_copy, u_copy, og_copy = [
        pltpu.make_async_copy(source, target, sems.at[k])
        for k, (source, target) in enumerate(
            ((w1_hbm, w1_ref), (w2_hbm, w2_ref), (pre_hbm, pre_ref), (u_hbm, u_ref), (og_hbm, og_ref))
        )
    ]
    for copy in (w1_copy, w2_copy, pre_copy, u_copy, og_copy):
        copy.start()
    w1_copy.wait()
    zero = jnp.zeros((CIN, C1), BF)
    for kx in range(3):
        for ky in range(3):
            at = SLOT[ky] * 2 * CIN
            r1_ref[kx, at : at + CIN, 0:C1] = w1_ref[kx, ky, 1]
            r1_ref[kx, at : at + CIN, C1:] = zero
            r1_ref[kx, at + CIN : at + 2 * CIN, 0:C1] = w1_ref[kx, ky, 2]
            r1_ref[kx, at + CIN : at + 2 * CIN, C1:] = w1_ref[kx, ky, 0]

    w2_copy.wait()
    zero = jnp.zeros((C1, C2), BF)
    for kx in range(3):
        for ky in range(3):
            t = kx * 3 + ky
            r2_ref[t, 0:C1, 0:C2] = w2_ref[kx, ky, 1]
            r2_ref[t, 0:C1, C2:] = zero
            r2_ref[t, C1:, 0:C2] = w2_ref[kx, ky, 2]
            r2_ref[t, C1:, C2:] = w2_ref[kx, ky, 0]

    pre_copy.wait()
    own = MY * MZ
    for mx in range(MX):
        pre = pre_ref[0, mx].reshape(own, C1).astype(F32)
        act_s[mx * own : (mx + 1) * own, :] = jnp.where(pre > 0, pre, 0.3 * pre)
    for px in range(2):
        for py in range(2):
            for s in range(2):
                rows = [
                    act_s[pl.ds((px * MY + 2 * j + py) * MZ + s, CZ, stride=2), :]
                    for j in range(CY)
                ]
                u2t_ref[px * 2 + py, s * C1 : (s + 1) * C1, :] = jnp.concatenate(rows, 0).T.astype(BF)

    u_copy.wait()
    for px in range(2):
        for py in range(2):
            for i in range(MX):
                for j in range(0, MY, 2):
                    pair = jnp.concatenate(
                        [u_ref[0, 2 * i + px, 2 * (j + e) + py] for e in range(2)], 0
                    )
                    at = (i * MY + j) * MZ
                    u1t_ref[px * 2 + py, :, at : at + 2 * MZ] = pair.T
    og_copy.wait()


def main_kernel(
    pre_ref, og_ref, hx_ref, hy_ref, hc_ref, r2_ref, u1t_ref, u2t_ref,
    a_ref, keep_ref, send_ref,
    b_s, ga_s, buf_s,
):
    def put_b(at, value):
        n = value.shape[0]
        b_s[at : at + n, 0:C2] = value
        b_s[at : at + n, C2:] = next_row(value.astype(F32), CZ).astype(BF)

    def inside(value, edge):
        return jnp.where(edge > 0, 0.0, value.astype(F32)).astype(BF)

    edge_x = (lax.axis_index(AX) == lax.axis_size(AX) - 1).astype(jnp.int32)
    edge_y = (lax.axis_index(AZ) == lax.axis_size(AZ) - 1).astype(jnp.int32)
    put_b(0, og_ref[0, 0].reshape(CY * CZ, C2))
    put_b(CY * CZ, inside(hy_ref[0:CZ], edge_y))
    put_b((CY + 1) * CZ, inside(hx_ref[0 : CY * CZ], edge_x))
    put_b((2 * CY + 1) * CZ, inside(hc_ref[0:CZ], edge_x + edge_y))

    def put_ga(mx, my, value):
        base = (mx * EY + my) * MZ
        ga_s[pl.ds(base, CZ, stride=2), :] = value[:, 0:C1]
        ga_s[pl.ds(base + 1, CZ, stride=2), :] = value[:, C1:]

    def b_rows(i, j, n):
        at = (i * (CY + 1) + j) * CZ
        return b_s[at : at + n * CZ, :]

    for px in range(2):
        for i in range(2 - px):
            for py in range(2):
                n = CY + 1 - py
                total = None
                for kx, dx in TAPS[px]:
                    for ky, dy in TAPS[py]:
                        part = nt(b_rows(i + dx, dy, n), r2_ref[kx * 3 + ky])
                        total = part if total is None else total + part
                for j in range(n):
                    put_ga(2 * i + px, 2 * j + py, total[j * CZ : (j + 1) * CZ])

    def put_a(at, pre):
        n = pre.shape[0]
        slope = jnp.where(pre.astype(F32) > 0, 1.0, 0.3)
        value = ga_s[at : at + n, :] * slope
        a_ref[at : at + n, 0:C1] = value.astype(BF)
        a_ref[at : at + n, C1:] = next_row(value, MZ).astype(BF)

    own = MY * MZ
    for mx in range(MX):
        put_a(mx * EY * MZ, pre_ref[0, mx].reshape(own, C1))
        put_a((mx * EY + MY) * MZ, hy_ref[CZ + mx * MZ : CZ + (mx + 1) * MZ])
    put_a(MX * EY * MZ, hx_ref[CY * CZ : CY * CZ + own])
    put_a((MX * EY + MY) * MZ, hc_ref[CZ : CZ + MZ])

    buf_s[ROWS_ONE + ROWS_TWO :, :] = jnp.zeros((ROWS - ROWS_ONE - ROWS_TWO, C1), BF)
    for kx in range(3):
        px, dx = TAP[kx]
        for ky in range(3):
            py, dy = TAP[ky]
            d = nn(u2t_ref[px * 2 + py], b_rows(dx, dy, CY)) * SCALE_TWO
            at = ROWS_ONE + (kx * 3 + ky) * 3 * C1
            buf_s[at : at + C1, :] = d[C1:, C2:].astype(BF)
            buf_s[at + C1 : at + 2 * C1, :] = d[0:C1, 0:C2].astype(BF)
            buf_s[at + 2 * C1 : at + 3 * C1, :] = d[C1:, 0:C2].astype(BF)

    for kx in range(3):
        px, dx = TAP[kx]
        for ky in range(3):
            py, dy = TAP[ky]
            total = None
            for i in range(MX):
                at = ((i + dx) * EY + dy) * MZ
                part = nn(
                    u1t_ref[px * 2 + py, :, i * own : (i + 1) * own], a_ref[at : at + own, :]
                )
                total = part if total is None else total + part
            d = total * SCALE_ONE
            at = (kx * 3 + ky) * 3 * CIN
            buf_s[at : at + CIN, :] = d[CIN:, C1:].astype(BF)
            buf_s[at + CIN : at + 2 * CIN, :] = d[0:CIN, 0:C1].astype(BF)
            buf_s[at + 2 * CIN : at + 3 * CIN, :] = d[CIN:, 0:C1].astype(BF)

    core = lax.axis_index("core")
    keep_ref[...] = buf_s[pl.ds(pl.multiple_of(core * HALF, HALF), HALF), :]
    send_ref[...] = buf_s[pl.ds(pl.multiple_of((1 - core) * HALF, HALF), HALF), :]


def input_kernel(a_ref, r1_ref, out_ref):
    wide = 2 * CIN
    step = 4
    for i in range(MX):
        for px in range(2):
            for j in range(0, MY, step):
                both = None
                odd = None
                for kx, dx in TAPS[px]:
                    at = ((i + dx) * EY + j) * MZ
                    part = nt(a_ref[at : at + step * MZ, :], r1_ref[kx, 0 : 2 * wide, :])
                    both = part if both is None else both + part
                    part = nt(a_ref[at + MZ : at + (step + 1) * MZ, :], r1_ref[kx, 2 * wide :, :])
                    odd = part if odd is None else odd + part
                even = both[:, 0:wide].astype(BF)
                odd = (both[:, wide:] + odd).astype(BF)
                for e in range(step):
                    rows = slice(e * MZ, (e + 1) * MZ)
                    out_ref[0, 2 * i + px, 2 * (j + e)] = even[rows]
                    out_ref[0, 2 * i + px, 2 * (j + e) + 1] = odd[rows]


def output_kernel(second, half_ref, *refs):
    one_hbm, two_hbm, wide, sems = refs[-4:]
    low = HALF - ROWS_ONE
    high = ROWS_TWO - low

    def put(parts):
        copies = []
        for k, (at, rows, target, to) in enumerate(parts):
            wide[at : at + rows] = half_ref[at : at + rows].astype(F32)
            copies.append(
                pltpu.make_async_copy(
                    wide.at[pl.ds(at, rows)], target.at[pl.ds(to, rows)], sems.at[k]
                )
            )
            copies[-1].start()
        for copy in copies:
            copy.wait()

    @pl.when(lax.axis_index("core") == second)
    def _():
        put(((0, ROWS_ONE // 2, one_hbm, 0), (ROWS_ONE // 2, ROWS_ONE // 2, one_hbm, ROWS_ONE // 2), (ROWS_ONE, low, two_hbm, 0)))

    @pl.when(lax.axis_index("core") != second)
    def _():
        third = 792
        put(((0, third, two_hbm, low), (third, third, two_hbm, low + third), (2 * third, high - 2 * third, two_hbm, low + 2 * third)))


def vmem(n):
    return [pl.BlockSpec(memory_space=pltpu.VMEM)] * n


def hbm(n):
    return [pl.BlockSpec(memory_space=pltpu.HBM)] * n


def far(*arrays):
    return [pltpu.with_memory_space_constraint(x, pltpu.HBM) for x in arrays]


LIMIT = 20 * 1024 * 1024


def call(kernel, name, out, scratch, in_specs, flops, bytes_moved):
    return pl.pallas_call(
        kernel,
        out_shape=tuple(out),
        in_specs=in_specs,
        out_specs=tuple(vmem(len(out))),
        scratch_shapes=scratch,
        cost_estimate=pl.CostEstimate(flops=flops, bytes_accessed=bytes_moved, transcendentals=0),
        compiler_params=pltpu.CompilerParams(vmem_limit_bytes=LIMIT),
        name=name,
    )


def pack_call(pre, og):
    out = [pltpu.VMEM(((CY * CZ + MY * MZ), C1), BF), pltpu.VMEM((CZ + MX * MZ, C1), BF), pltpu.VMEM((CZ + MZ, C1), BF)]
    count = CY + MY + 1 + MX + 2
    return call(pack_kernel, "pack", out, [pltpu.SemaphoreType.DMA((count,))], hbm(2), 0, 500_000)(*far(pre, og))


def prep_call(u, pre, og, w1, w2):
    out = [
        pltpu.VMEM((3, 6 * CIN, 2 * C1), BF),
        pltpu.VMEM((9, 2 * C1, 2 * C2), BF),
        pltpu.VMEM((4, 2 * CIN, MX * MY * MZ), BF),
        pltpu.VMEM((4, 2 * C1, CY * CZ), BF),
        pltpu.VMEM(pre.shape, BF),
        pltpu.VMEM(og.shape, BF),
    ]
    scratch = [
        pltpu.VMEM(u.shape, BF),
        pltpu.VMEM(w1.shape, BF),
        pltpu.VMEM(w2.shape, BF),
        pltpu.VMEM((MX * MY * MZ, C1), F32),
        pltpu.SemaphoreType.DMA((5,)),
    ]
    return call(prep_kernel, "prep", out, scratch, hbm(5), 0, 6_000_000)(*far(u, pre, og, w1, w2))


def main_call(pre, og, hx, hy, hc, r2, u1t, u2t):
    out = [
        pltpu.VMEM((EX * EY * MZ, 2 * C1), BF),
        pltpu.VMEM((HALF, C1), BF),
        pltpu.VMEM((HALF, C1), BF),
    ]
    scratch = [
        pltpu.VMEM((2 * (CY + 1) * CZ, 2 * C2), BF),
        pltpu.VMEM((EX * EY * MZ, C1), F32),
        pltpu.VMEM((ROWS, C1), BF),
    ]
    return call(main_kernel, "main", out, scratch, vmem(8), 2_000_000_000, 8_000_000)(
        pre, og, hx, hy, hc, r2, u1t, u2t
    )


def input_call(a, r1):
    out = [jax.ShapeDtypeStruct((1, 2 * MX, 2 * MY, MZ, 2 * CIN), BF)]
    return call(input_kernel, "grad_input", out, [], vmem(2), 1_200_000_000, 3_000_000)(a, r1)[0]


def output_call(half, before=()):
    second = len(before) // 2
    return pl.pallas_call(
        functools.partial(output_kernel, second),
        out_shape=(
            jax.ShapeDtypeStruct((ROWS_ONE, C1), F32),
            jax.ShapeDtypeStruct((ROWS_TWO, C1), F32),
        ),
        in_specs=vmem(1) + hbm(len(before)),
        out_specs=tuple(hbm(2)),
        scratch_shapes=[pltpu.VMEM((HALF, C1), F32), pltpu.SemaphoreType.DMA((3,))],
        input_output_aliases={1: 0, 2: 1} if second else {},
        cost_estimate=pl.CostEstimate(flops=0, bytes_accessed=2_000_000, transcendentals=0),
        compiler_params=pltpu.CompilerParams(vmem_limit_bytes=LIMIT),
        name="output",
    )(half, *before)


def on_device(u, pre, og, w1, w2):
    sx = lax.axis_size("y") * lax.axis_size("xl")
    sz = lax.axis_size("zh") * lax.axis_size("zl")
    from_x = [((i + 1) % sx, i) for i in range(sx)]
    from_z = [((i + 1) % sz, i) for i in range(sz)]
    from_xz = [
        ((i + 1) % sx * sz + (j + 1) % sz, i * sz + j) for i in range(sx) for j in range(sz)
    ]
    hx, hy, hc = pack_call(pre, og)
    hx = lax.ppermute(hx, AX, from_x)
    hc = lax.ppermute(hc, AX + AZ, from_xz)
    hy = lax.ppermute(hy, AZ, from_z)
    r1, r2, u1t, u2t, pre, og = prep_call(u, pre, og, w1, w2)
    a, keep, send = main_call(pre, og, hx, hy, hc, r2, u1t, u2t)
    received = lax.ppermute(send, "core", [(0, 1), (1, 0)])
    grad_input = input_call(a, r1)
    received, grad_input = lax.optimization_barrier((received, grad_input))

    group = ("xh", "y", "xl", "zl")
    half = (keep.astype(F32) + received.astype(F32)).astype(BF).reshape(GROUP, CHUNK, C1)
    parts = lax.all_to_all(half, group, 0, 0, tiled=True)
    chunk = jnp.sum(parts.astype(F32), axis=0).astype(BF)
    parts = lax.all_to_all(jnp.broadcast_to(chunk[None], (4, CHUNK, C1)), "zh", 0, 0, tiled=True)
    chunk = jnp.sum(parts.astype(F32), axis=0).astype(BF)
    mine = lax.all_to_all(jnp.broadcast_to(chunk[None], (GROUP, CHUNK, C1)), group, 0, 0, tiled=True)
    mine = mine.reshape(HALF, C1)
    other = lax.ppermute(mine, "core", [(0, 1), (1, 0)])
    grad_one, grad_two = output_call(other, output_call(mine))
    return grad_input, grad_one.reshape(3, 3, 3, CIN, C1), grad_two.reshape(3, 3, 3, C1, C2)


def solution(mesh):
    fine = Mesh(mesh.devices.reshape(2, 2, 4, 2, 4, 2), ("xh", "core", "y", "xl", "zh", "zl"))
    spec = P(("xh", "core"), ("y", "xl"), ("zh", "zl"), None, None)
    return jax.shard_map(
        on_device,
        mesh=fine,
        in_specs=(spec, spec, spec, P(), P()),
        out_specs=(spec, P(), P()),
        check_vma=False,
    )
```

```python
import functools

import jax
import jax.numpy as jnp
from jax import lax
from jax.experimental import pallas as pl
from jax.experimental.pallas import tpu as pltpu
from jax.sharding import Mesh
from jax.sharding import PartitionSpec as P


BF = jnp.bfloat16
F32 = jnp.float32

CY, CZ = 4, 32
MX, MY, MZ = 2, 8, 64
CIN, C1, C2 = 64, 128, 128
EX, EY = MX + 1, MY + 1
CHUNK = 88
AX = ("y", "xl")
AZ = ("zh", "zl")
GROUP = 32
HALF = CHUNK * GROUP
ROWS_ONE = 27 * CIN
ROWS_TWO = 27 * C1
SCALE_ONE = float(4 * 16 * 64 * 64) ** (-0.5)
SCALE_TWO = float(4 * 8 * 32 * 32) ** (-0.5)

TAP = ((1, 1), (0, 0), (1, 0))
TAPS = (((1, 0),), ((2, 0), (0, 1)))
SLOT = (2, 0, 1)


def nt(a, b):
    return lax.dot_general(a, b, (((1,), (1,)), ((), ())), preferred_element_type=F32)


def nn(a, b):
    return lax.dot_general(a, b, (((1,), (0,)), ((), ())), preferred_element_type=F32)


def next_row(value, period):
    rows = value.shape[0]
    rolled = pltpu.roll(value, rows - 1, 0)
    row = lax.broadcasted_iota(jnp.int32, value.shape, 0)
    return jnp.where(row % period == period - 1, 0.0, rolled)


def pack_kernel(pre_ref, og_ref, hx_ref, hy_ref, hc_ref, sems):
    copies = []

    def copy(src, dst):
        copies.append(pltpu.make_async_copy(src, dst, sems.at[len(copies)]))
        copies[-1].start()

    for j in range(CY):
        copy(og_ref.at[0, 0, j], hx_ref.at[pl.ds(j * CZ, CZ)])
    for y in range(MY):
        copy(pre_ref.at[0, 0, y], hx_ref.at[pl.ds(CY * CZ + y * MZ, MZ)])
    copy(og_ref.at[0, 0, 0], hy_ref.at[pl.ds(0, CZ)])
    for x in range(MX):
        copy(pre_ref.at[0, x, 0], hy_ref.at[pl.ds(CZ + x * MZ, MZ)])
    copy(og_ref.at[0, 0, 0], hc_ref.at[pl.ds(0, CZ)])
    copy(pre_ref.at[0, 0, 0], hc_ref.at[pl.ds(CZ, MZ)])
    for c in copies:
        c.wait()


def prep_kernel(
    u_hbm, pre_hbm, og_hbm, w1_hbm, w2_hbm,
    r1_ref, r2_ref, u1t_ref, u2t_ref, pre_ref, og_ref,
    u_ref, w1_ref, w2_ref, act_s, sems,
):
    w1_copy, w2_copy, pre_copy, u_copy, og_copy = [
        pltpu.make_async_copy(source, target, sems.at[k])
        for k, (source, target) in enumerate(
            ((w1_hbm, w1_ref), (w2_hbm, w2_ref), (pre_hbm, pre_ref), (u_hbm, u_ref), (og_hbm, og_ref))
        )
    ]
    for copy in (w1_copy, w2_copy, pre_copy, u_copy, og_copy):
        copy.start()
    w1_copy.wait()
    zero = jnp.zeros((CIN, C1), BF)
    for kx in range(3):
        for ky in range(3):
            at = SLOT[ky] * 2 * CIN
            r1_ref[kx, at : at + CIN, 0:C1] = w1_ref[kx, ky, 1]
            r1_ref[kx, at : at + CIN, C1:] = zero
            r1_ref[kx, at + CIN : at + 2 * CIN, 0:C1] = w1_ref[kx, ky, 2]
            r1_ref[kx, at + CIN : at + 2 * CIN, C1:] = w1_ref[kx, ky, 0]

    w2_copy.wait()
    zero = jnp.zeros((C1, C2), BF)
    for kx in range(3):
        for ky in range(3):
            t = kx * 3 + ky
            r2_ref[t, 0:C1, 0:C2] = w2_ref[kx, ky, 1]
            r2_ref[t, 0:C1, C2:] = zero
            r2_ref[t, C1:, 0:C2] = w2_ref[kx, ky, 2]
            r2_ref[t, C1:, C2:] = w2_ref[kx, ky, 0]

    pre_copy.wait()
    own = MY * MZ
    for mx in range(MX):
        pre = pre_ref[0, mx].reshape(own, C1).astype(F32)
        act_s[mx * own : (mx + 1) * own, :] = jnp.where(pre > 0, pre, 0.3 * pre)
    for px in range(2):
        for py in range(2):
            for s in range(2):
                rows = [
                    act_s[pl.ds((px * MY + 2 * j + py) * MZ + s, CZ, stride=2), :]
                    for j in range(CY)
                ]
                u2t_ref[px * 2 + py, s * C1 : (s + 1) * C1, :] = jnp.concatenate(rows, 0).T.astype(BF)

    u_copy.wait()
    for px in range(2):
        for py in range(2):
            for i in range(MX):
                for j in range(0, MY, 2):
                    pair = jnp.concatenate(
                        [u_ref[0, 2 * i + px, 2 * (j + e) + py] for e in range(2)], 0
                    )
                    at = (i * MY + j) * MZ
                    u1t_ref[px * 2 + py, :, at : at + 2 * MZ] = pair.T
    og_copy.wait()


def share(buf_s, keep_ref, send_ref, rows):
    core = lax.axis_index("core")
    keep_ref[...] = buf_s[pl.ds(pl.multiple_of(core * rows, rows), rows), :]
    send_ref[...] = buf_s[pl.ds(pl.multiple_of((1 - core) * rows, rows), rows), :]


def main_kernel(
    pre_ref, og_ref, hx_ref, hy_ref, hc_ref, r2_ref, u2t_ref,
    a_ref, keep_ref, send_ref,
    b_s, ga_s, buf_s,
):
    def put_b(at, value):
        n = value.shape[0]
        b_s[at : at + n, 0:C2] = value
        b_s[at : at + n, C2:] = next_row(value.astype(F32), CZ).astype(BF)

    def inside(value, edge):
        return jnp.where(edge > 0, 0.0, value.astype(F32)).astype(BF)

    edge_x = (lax.axis_index(AX) == lax.axis_size(AX) - 1).astype(jnp.int32)
    edge_y = (lax.axis_index(AZ) == lax.axis_size(AZ) - 1).astype(jnp.int32)
    put_b(0, og_ref[0, 0].reshape(CY * CZ, C2))
    put_b(CY * CZ, inside(hy_ref[0:CZ], edge_y))
    put_b((CY + 1) * CZ, inside(hx_ref[0 : CY * CZ], edge_x))
    put_b((2 * CY + 1) * CZ, inside(hc_ref[0:CZ], edge_x + edge_y))

    def put_ga(mx, my, value):
        base = (mx * EY + my) * MZ
        ga_s[pl.ds(base, CZ, stride=2), :] = value[:, 0:C1]
        ga_s[pl.ds(base + 1, CZ, stride=2), :] = value[:, C1:]

    def b_rows(i, j, n):
        at = (i * (CY + 1) + j) * CZ
        return b_s[at : at + n * CZ, :]

    for px in range(2):
        for i in range(2 - px):
            for py in range(2):
                n = CY + 1 - py
                total = None
                for kx, dx in TAPS[px]:
                    for ky, dy in TAPS[py]:
                        part = nt(b_rows(i + dx, dy, n), r2_ref[kx * 3 + ky])
                        total = part if total is None else total + part
                for j in range(n):
                    put_ga(2 * i + px, 2 * j + py, total[j * CZ : (j + 1) * CZ])

    def put_a(at, pre):
        n = pre.shape[0]
        slope = jnp.where(pre.astype(F32) > 0, 1.0, 0.3)
        value = ga_s[at : at + n, :] * slope
        a_ref[at : at + n, 0:C1] = value.astype(BF)
        a_ref[at : at + n, C1:] = next_row(value, MZ).astype(BF)

    own = MY * MZ
    for mx in range(MX):
        put_a(mx * EY * MZ, pre_ref[0, mx].reshape(own, C1))
        put_a((mx * EY + MY) * MZ, hy_ref[CZ + mx * MZ : CZ + (mx + 1) * MZ])
    put_a(MX * EY * MZ, hx_ref[CY * CZ : CY * CZ + own])
    put_a((MX * EY + MY) * MZ, hc_ref[CZ : CZ + MZ])

    for kx in range(3):
        px, dx = TAP[kx]
        for ky in range(3):
            py, dy = TAP[ky]
            d = nn(u2t_ref[px * 2 + py], b_rows(dx, dy, CY)) * SCALE_TWO
            at = (kx * 3 + ky) * 3 * C1
            buf_s[at : at + C1, :] = d[C1:, C2:].astype(BF)
            buf_s[at + C1 : at + 2 * C1, :] = d[0:C1, 0:C2].astype(BF)
            buf_s[at + 2 * C1 : at + 3 * C1, :] = d[C1:, 0:C2].astype(BF)

    share(buf_s, keep_ref, send_ref, ROWS_TWO // 2)


def one_kernel(a_ref, u1t_ref, keep_ref, send_ref, buf_s):
    own = MY * MZ
    for kx in range(3):
        px, dx = TAP[kx]
        for ky in range(3):
            py, dy = TAP[ky]
            total = None
            for i in range(MX):
                at = ((i + dx) * EY + dy) * MZ
                part = nn(
                    u1t_ref[px * 2 + py, :, i * own : (i + 1) * own], a_ref[at : at + own, :]
                )
                total = part if total is None else total + part
            d = total * SCALE_ONE
            at = (kx * 3 + ky) * 3 * CIN
            buf_s[at : at + CIN, :] = d[CIN:, C1:].astype(BF)
            buf_s[at + CIN : at + 2 * CIN, :] = d[0:CIN, 0:C1].astype(BF)
            buf_s[at + 2 * CIN : at + 3 * CIN, :] = d[CIN:, 0:C1].astype(BF)

    share(buf_s, keep_ref, send_ref, ROWS_ONE // 2)


def join_kernel(keep_two, got_two, keep_one, got_one, half_ref):
    two = ROWS_TWO // 2
    both = two + ROWS_ONE // 2
    half_ref[0:two] = (keep_two[...].astype(F32) + got_two[...].astype(F32)).astype(BF)
    half_ref[two:both] = (keep_one[...].astype(F32) + got_one[...].astype(F32)).astype(BF)
    half_ref[both:] = jnp.zeros((HALF - both, C1), BF)


def input_kernel(a_ref, r1_ref, out_ref):
    wide = 2 * CIN
    step = 4
    for i in range(MX):
        for px in range(2):
            for j in range(0, MY, step):
                both = None
                odd = None
                for kx, dx in TAPS[px]:
                    at = ((i + dx) * EY + j) * MZ
                    part = nt(a_ref[at : at + step * MZ, :], r1_ref[kx, 0 : 2 * wide, :])
                    both = part if both is None else both + part
                    part = nt(a_ref[at + MZ : at + (step + 1) * MZ, :], r1_ref[kx, 2 * wide :, :])
                    odd = part if odd is None else odd + part
                even = both[:, 0:wide].astype(BF)
                odd = (both[:, wide:] + odd).astype(BF)
                for e in range(step):
                    rows = slice(e * MZ, (e + 1) * MZ)
                    out_ref[0, 2 * i + px, 2 * (j + e)] = even[rows]
                    out_ref[0, 2 * i + px, 2 * (j + e) + 1] = odd[rows]


def output_kernel(second, half_ref, *refs):
    one_hbm, two_hbm, wide, sems = refs[-4:]
    core = lax.axis_index("core")
    core = 1 - core if second else core
    copies = []
    for k in range(3):
        target, rows = ((two_hbm, ROWS_TWO // 4), (two_hbm, ROWS_TWO // 4), (one_hbm, ROWS_ONE // 2))[k]
        at = k * (ROWS_TWO // 4)
        wide[at : at + rows] = half_ref[at : at + rows].astype(F32)
        start = core * (ROWS_TWO // 2) + at if k < 2 else core * rows
        copies.append(
            pltpu.make_async_copy(
                wide.at[pl.ds(at, rows)],
                target.at[pl.ds(pl.multiple_of(start, 8), rows)],
                sems.at[k],
            )
        )
        copies[-1].start()
    for copy in copies:
        copy.wait()


def vmem(n):
    return [pl.BlockSpec(memory_space=pltpu.VMEM)] * n


def hbm(n):
    return [pl.BlockSpec(memory_space=pltpu.HBM)] * n


def far(*arrays):
    return [pltpu.with_memory_space_constraint(x, pltpu.HBM) for x in arrays]


LIMIT = 20 * 1024 * 1024


def call(kernel, out, scratch, in_specs, flops, bytes_moved):
    return pl.pallas_call(
        kernel,
        out_shape=tuple(out),
        in_specs=in_specs,
        out_specs=tuple(vmem(len(out))),
        scratch_shapes=scratch,
        cost_estimate=pl.CostEstimate(flops=flops, bytes_accessed=bytes_moved, transcendentals=0),
        compiler_params=pltpu.CompilerParams(vmem_limit_bytes=LIMIT),
    )


def pack_call(pre, og):
    out = [pltpu.VMEM(((CY * CZ + MY * MZ), C1), BF), pltpu.VMEM((CZ + MX * MZ, C1), BF), pltpu.VMEM((CZ + MZ, C1), BF)]
    count = CY + MY + 1 + MX + 2
    return call(pack_kernel, out, [pltpu.SemaphoreType.DMA((count,))], hbm(2), 0, 500_000)(*far(pre, og))


def prep_call(u, pre, og, w1, w2):
    out = [
        pltpu.VMEM((3, 6 * CIN, 2 * C1), BF),
        pltpu.VMEM((9, 2 * C1, 2 * C2), BF),
        pltpu.VMEM((4, 2 * CIN, MX * MY * MZ), BF),
        pltpu.VMEM((4, 2 * C1, CY * CZ), BF),
        pltpu.VMEM(pre.shape, BF),
        pltpu.VMEM(og.shape, BF),
    ]
    scratch = [
        pltpu.VMEM(u.shape, BF),
        pltpu.VMEM(w1.shape, BF),
        pltpu.VMEM(w2.shape, BF),
        pltpu.VMEM((MX * MY * MZ, C1), F32),
        pltpu.SemaphoreType.DMA((5,)),
    ]
    return call(prep_kernel, out, scratch, hbm(5), 0, 6_000_000)(*far(u, pre, og, w1, w2))


def main_call(pre, og, hx, hy, hc, r2, u2t):
    out = [
        pltpu.VMEM((EX * EY * MZ, 2 * C1), BF),
        pltpu.VMEM((ROWS_TWO // 2, C1), BF),
        pltpu.VMEM((ROWS_TWO // 2, C1), BF),
    ]
    scratch = [
        pltpu.VMEM((2 * (CY + 1) * CZ, 2 * C2), BF),
        pltpu.VMEM((EX * EY * MZ, C1), F32),
        pltpu.VMEM((ROWS_TWO, C1), BF),
    ]
    return call(main_kernel, out, scratch, vmem(7), 800_000_000, 4_000_000)(
        pre, og, hx, hy, hc, r2, u2t
    )


def one_call(a, u1t):
    out = [pltpu.VMEM((ROWS_ONE // 2, C1), BF), pltpu.VMEM((ROWS_ONE // 2, C1), BF)]
    scratch = [pltpu.VMEM((ROWS_ONE, C1), BF)]
    return call(one_kernel, out, scratch, vmem(2), 1_200_000_000, 3_000_000)(a, u1t)


def join_call(*parts):
    return call(join_kernel, [pltpu.VMEM((HALF, C1), BF)], [], vmem(4), 0, 2_000_000)(*parts)[0]


def input_call(a, r1):
    out = [jax.ShapeDtypeStruct((1, 2 * MX, 2 * MY, MZ, 2 * CIN), BF)]
    return call(input_kernel, out, [], vmem(2), 1_200_000_000, 3_000_000)(a, r1)[0]


def output_call(half, before=()):
    second = len(before) // 2
    return pl.pallas_call(
        functools.partial(output_kernel, second),
        out_shape=(
            jax.ShapeDtypeStruct((ROWS_ONE, C1), F32),
            jax.ShapeDtypeStruct((ROWS_TWO, C1), F32),
        ),
        in_specs=vmem(1) + hbm(len(before)),
        out_specs=tuple(hbm(2)),
        scratch_shapes=[pltpu.VMEM((HALF, C1), F32), pltpu.SemaphoreType.DMA((3,))],
        input_output_aliases={1: 0, 2: 1} if second else {},
        cost_estimate=pl.CostEstimate(flops=0, bytes_accessed=2_000_000, transcendentals=0),
        compiler_params=pltpu.CompilerParams(vmem_limit_bytes=LIMIT),
        name="output",
    )(half, *before)


def backward(u, pre, og, w1, w2):
    sx = lax.axis_size("y") * lax.axis_size("xl")
    sz = lax.axis_size("zh") * lax.axis_size("zl")
    from_x = [((i + 1) % sx, i) for i in range(sx)]
    from_z = [((i + 1) % sz, i) for i in range(sz)]
    from_xz = [
        ((i + 1) % sx * sz + (j + 1) % sz, i * sz + j) for i in range(sx) for j in range(sz)
    ]
    hx, hy, hc = pack_call(pre, og)
    hx = lax.ppermute(hx, AX, from_x)
    hc = lax.ppermute(hc, AX + AZ, from_xz)
    hy = lax.ppermute(hy, AZ, from_z)
    r1, r2, u1t, u2t, pre, og = prep_call(u, pre, og, w1, w2)
    swap = [(0, 1), (1, 0)]
    a, keep_two, send_two = main_call(pre, og, hx, hy, hc, r2, u2t)
    got_two = lax.ppermute(send_two, "core", swap)
    keep_one, send_one = one_call(a, u1t)
    got_one = lax.ppermute(send_one, "core", swap)
    half = join_call(keep_two, got_two, keep_one, got_one)

    group = ("xh", "xl", "zl", "y")
    parts = lax.all_to_all(half.reshape(GROUP, CHUNK, C1), group, 0, 0, tiled=True)
    grad_input = input_call(a, r1)
    chunk = jnp.sum(parts.astype(F32), axis=0).astype(BF)
    far = lax.ppermute(chunk, "zh", [((i + 2) % 4, i) for i in range(4)])
    up = lax.ppermute(chunk, "zh", [((i + 1) % 4, i) for i in range(4)])
    down = lax.ppermute(chunk, "zh", [((i + 3) % 4, i) for i in range(4)])
    chunk = (chunk.astype(F32) + far.astype(F32)) + (up.astype(F32) + down.astype(F32))
    chunk = jnp.broadcast_to(chunk.astype(BF)[None], (GROUP, CHUNK, C1))
    mine = lax.all_to_all(chunk, group, 0, 0, tiled=True).reshape(HALF, C1)
    other = lax.ppermute(mine, "core", swap)
    grad_one, grad_two = output_call(other, output_call(mine))
    return grad_input, grad_one.reshape(3, 3, 3, CIN, C1), grad_two.reshape(3, 3, 3, C1, C2)


def solution(mesh):
    fine = Mesh(mesh.devices.reshape(2, 2, 4, 2, 4, 2), ("xh", "core", "y", "xl", "zh", "zl"))
    spec = P(("xh", "core"), ("y", "xl"), ("zh", "zl"), None, None)
    return jax.shard_map(
        backward,
        mesh=fine,
        in_specs=(spec, spec, spec, P(), P()),
        out_specs=(spec, P(), P()),
        check_vma=False,
    )
```

```python
import functools

import jax
import jax.numpy as jnp
from jax import lax
from jax.experimental import pallas as pl
from jax.experimental.pallas import tpu as pltpu
from jax.sharding import Mesh
from jax.sharding import PartitionSpec as P


BF = jnp.bfloat16
F32 = jnp.float32

CY, CZ = 4, 32
MX, MY, MZ = 2, 8, 64
CIN, C1, C2 = 64, 128, 128
EX, EY = MX + 1, MY + 1
CHUNK = 88
AX = ("y", "xl")
AZ = ("zh", "zl")
GROUP = 32
HALF = CHUNK * GROUP
ROWS_ONE = 27 * CIN
ROWS_TWO = 27 * C1
SCALE_ONE = float(4 * 16 * 64 * 64) ** (-0.5)
SCALE_TWO = float(4 * 8 * 32 * 32) ** (-0.5)

TAP = ((1, 1), (0, 0), (1, 0))
TAPS = (((1, 0),), ((2, 0), (0, 1)))
SLOT = (2, 0, 1)


def nt(a, b):
    return lax.dot_general(a, b, (((1,), (1,)), ((), ())), preferred_element_type=F32)


def nn(a, b):
    return lax.dot_general(a, b, (((1,), (0,)), ((), ())), preferred_element_type=F32)


def next_row(value, period):
    rows = value.shape[0]
    rolled = pltpu.roll(value, rows - 1, 0)
    row = lax.broadcasted_iota(jnp.int32, value.shape, 0)
    return jnp.where(row % period == period - 1, 0.0, rolled)


def pack_kernel(pre_ref, og_ref, hx_ref, hy_ref, hc_ref, sems):
    copies = []

    def copy(src, dst):
        copies.append(pltpu.make_async_copy(src, dst, sems.at[len(copies)]))
        copies[-1].start()

    for j in range(CY):
        copy(og_ref.at[0, 0, j], hx_ref.at[pl.ds(j * CZ, CZ)])
    for y in range(MY):
        copy(pre_ref.at[0, 0, y], hx_ref.at[pl.ds(CY * CZ + y * MZ, MZ)])
    copy(og_ref.at[0, 0, 0], hy_ref.at[pl.ds(0, CZ)])
    for x in range(MX):
        copy(pre_ref.at[0, x, 0], hy_ref.at[pl.ds(CZ + x * MZ, MZ)])
    copy(og_ref.at[0, 0, 0], hc_ref.at[pl.ds(0, CZ)])
    copy(pre_ref.at[0, 0, 0], hc_ref.at[pl.ds(CZ, MZ)])
    for c in copies:
        c.wait()


def prep_kernel(
    u_hbm, pre_hbm, og_hbm, w1_hbm, w2_hbm,
    r1_ref, r2_ref, u1t_ref, u2t_ref, pre_ref, og_ref,
    u_ref, w1_ref, w2_ref, act_s, sems,
):
    w1_copy, w2_copy, pre_copy, u_copy, og_copy = [
        pltpu.make_async_copy(source, target, sems.at[k])
        for k, (source, target) in enumerate(
            ((w1_hbm, w1_ref), (w2_hbm, w2_ref), (pre_hbm, pre_ref), (u_hbm, u_ref), (og_hbm, og_ref))
        )
    ]
    for copy in (w1_copy, w2_copy, pre_copy, u_copy, og_copy):
        copy.start()
    w1_copy.wait()
    zero = jnp.zeros((CIN, C1), BF)
    for kx in range(3):
        for ky in range(3):
            at = SLOT[ky] * 2 * CIN
            r1_ref[kx, at : at + CIN, 0:C1] = w1_ref[kx, ky, 1]
            r1_ref[kx, at : at + CIN, C1:] = zero
            r1_ref[kx, at + CIN : at + 2 * CIN, 0:C1] = w1_ref[kx, ky, 2]
            r1_ref[kx, at + CIN : at + 2 * CIN, C1:] = w1_ref[kx, ky, 0]

    w2_copy.wait()
    zero = jnp.zeros((C1, C2), BF)
    for kx in range(3):
        for ky in range(3):
            t = kx * 3 + ky
            r2_ref[t, 0:C1, 0:C2] = w2_ref[kx, ky, 1]
            r2_ref[t, 0:C1, C2:] = zero
            r2_ref[t, C1:, 0:C2] = w2_ref[kx, ky, 2]
            r2_ref[t, C1:, C2:] = w2_ref[kx, ky, 0]

    pre_copy.wait()
    own = MY * MZ
    for mx in range(MX):
        pre = pre_ref[0, mx].reshape(own, C1).astype(F32)
        act_s[mx * own : (mx + 1) * own, :] = jnp.where(pre > 0, pre, 0.3 * pre)
    for px in range(2):
        for py in range(2):
            for s in range(2):
                rows = [
                    act_s[pl.ds((px * MY + 2 * j + py) * MZ + s, CZ, stride=2), :]
                    for j in range(CY)
                ]
                u2t_ref[px * 2 + py, s * C1 : (s + 1) * C1, :] = jnp.concatenate(rows, 0).T.astype(BF)

    u_copy.wait()
    for px in range(2):
        for py in range(2):
            for i in range(MX):
                for j in range(0, MY, 2):
                    pair = jnp.concatenate(
                        [u_ref[0, 2 * i + px, 2 * (j + e) + py] for e in range(2)], 0
                    )
                    at = (i * MY + j) * MZ
                    u1t_ref[px * 2 + py, :, at : at + 2 * MZ] = pair.T
    og_copy.wait()


def share(buf_s, keep_ref, send_ref, rows):
    core = lax.axis_index("core")
    keep_ref[...] = buf_s[pl.ds(pl.multiple_of(core * rows, rows), rows), :]
    send_ref[...] = buf_s[pl.ds(pl.multiple_of((1 - core) * rows, rows), rows), :]


def main_kernel(
    pre_ref, og_ref, hx_ref, hy_ref, hc_ref, r2_ref, u2t_ref,
    a_ref, keep_ref, send_ref,
    b_s, ga_s, buf_s,
):
    def put_b(at, value):
        n = value.shape[0]
        b_s[at : at + n, 0:C2] = value
        b_s[at : at + n, C2:] = next_row(value.astype(F32), CZ).astype(BF)

    def inside(value, edge):
        return jnp.where(edge > 0, 0.0, value.astype(F32)).astype(BF)

    edge_x = (lax.axis_index(AX) == lax.axis_size(AX) - 1).astype(jnp.int32)
    edge_y = (lax.axis_index(AZ) == lax.axis_size(AZ) - 1).astype(jnp.int32)
    put_b(0, og_ref[0, 0].reshape(CY * CZ, C2))
    put_b(CY * CZ, inside(hy_ref[0:CZ], edge_y))
    put_b((CY + 1) * CZ, inside(hx_ref[0 : CY * CZ], edge_x))
    put_b((2 * CY + 1) * CZ, inside(hc_ref[0:CZ], edge_x + edge_y))

    def put_ga(mx, my, value):
        base = (mx * EY + my) * MZ
        ga_s[pl.ds(base, CZ, stride=2), :] = value[:, 0:C1]
        ga_s[pl.ds(base + 1, CZ, stride=2), :] = value[:, C1:]

    def b_rows(i, j, n):
        at = (i * (CY + 1) + j) * CZ
        return b_s[at : at + n * CZ, :]

    for px in range(2):
        for i in range(2 - px):
            for py in range(2):
                n = CY + 1 - py
                total = None
                for kx, dx in TAPS[px]:
                    for ky, dy in TAPS[py]:
                        part = nt(b_rows(i + dx, dy, n), r2_ref[kx * 3 + ky])
                        total = part if total is None else total + part
                for j in range(n):
                    put_ga(2 * i + px, 2 * j + py, total[j * CZ : (j + 1) * CZ])

    def put_a(at, pre):
        n = pre.shape[0]
        slope = jnp.where(pre.astype(F32) > 0, 1.0, 0.3)
        value = ga_s[at : at + n, :] * slope
        a_ref[at : at + n, 0:C1] = value.astype(BF)
        a_ref[at : at + n, C1:] = next_row(value, MZ).astype(BF)

    own = MY * MZ
    for mx in range(MX):
        put_a(mx * EY * MZ, pre_ref[0, mx].reshape(own, C1))
        put_a((mx * EY + MY) * MZ, hy_ref[CZ + mx * MZ : CZ + (mx + 1) * MZ])
    put_a(MX * EY * MZ, hx_ref[CY * CZ : CY * CZ + own])
    put_a((MX * EY + MY) * MZ, hc_ref[CZ : CZ + MZ])

    for kx in range(3):
        px, dx = TAP[kx]
        for ky in range(3):
            py, dy = TAP[ky]
            d = nn(u2t_ref[px * 2 + py], b_rows(dx, dy, CY)) * SCALE_TWO
            at = (kx * 3 + ky) * 3 * C1
            buf_s[at : at + C1, :] = d[C1:, C2:].astype(BF)
            buf_s[at + C1 : at + 2 * C1, :] = d[0:C1, 0:C2].astype(BF)
            buf_s[at + 2 * C1 : at + 3 * C1, :] = d[C1:, 0:C2].astype(BF)

    share(buf_s, keep_ref, send_ref, ROWS_TWO // 2)


def one_kernel(a_ref, u1t_ref, keep_ref, send_ref, buf_s):
    own = MY * MZ
    for kx in range(3):
        px, dx = TAP[kx]
        for ky in range(3):
            py, dy = TAP[ky]
            total = None
            for i in range(MX):
                at = ((i + dx) * EY + dy) * MZ
                part = nn(
                    u1t_ref[px * 2 + py, :, i * own : (i + 1) * own], a_ref[at : at + own, :]
                )
                total = part if total is None else total + part
            d = total * SCALE_ONE
            at = (kx * 3 + ky) * 3 * CIN
            buf_s[at : at + CIN, :] = d[CIN:, C1:].astype(BF)
            buf_s[at + CIN : at + 2 * CIN, :] = d[0:CIN, 0:C1].astype(BF)
            buf_s[at + 2 * CIN : at + 3 * CIN, :] = d[CIN:, 0:C1].astype(BF)

    share(buf_s, keep_ref, send_ref, ROWS_ONE // 2)


def join_kernel(keep_two, got_two, keep_one, got_one, half_ref):
    two = ROWS_TWO // 2
    both = two + ROWS_ONE // 2
    half_ref[0:two] = (keep_two[...].astype(F32) + got_two[...].astype(F32)).astype(BF)
    half_ref[two:both] = (keep_one[...].astype(F32) + got_one[...].astype(F32)).astype(BF)
    half_ref[both:] = jnp.zeros((HALF - both, C1), BF)


def input_kernel(a_ref, r1_ref, out_ref):
    wide = 2 * CIN
    step = 4
    for i in range(MX):
        for px in range(2):
            for j in range(0, MY, step):
                both = None
                odd = None
                for kx, dx in TAPS[px]:
                    at = ((i + dx) * EY + j) * MZ
                    part = nt(a_ref[at : at + step * MZ, :], r1_ref[kx, 0 : 2 * wide, :])
                    both = part if both is None else both + part
                    part = nt(a_ref[at + MZ : at + (step + 1) * MZ, :], r1_ref[kx, 2 * wide :, :])
                    odd = part if odd is None else odd + part
                even = both[:, 0:wide].astype(BF)
                odd = (both[:, wide:] + odd).astype(BF)
                for e in range(step):
                    rows = slice(e * MZ, (e + 1) * MZ)
                    out_ref[0, 2 * i + px, 2 * (j + e)] = even[rows]
                    out_ref[0, 2 * i + px, 2 * (j + e) + 1] = odd[rows]


def output_kernel(second, half_ref, *refs):
    one_hbm, two_hbm, wide, sems = refs[-4:]
    core = lax.axis_index("core")
    core = 1 - core if second else core
    copies = []
    for k in range(3):
        target, rows = ((two_hbm, ROWS_TWO // 4), (two_hbm, ROWS_TWO // 4), (one_hbm, ROWS_ONE // 2))[k]
        at = k * (ROWS_TWO // 4)
        wide[at : at + rows] = half_ref[at : at + rows].astype(F32)
        start = core * (ROWS_TWO // 2) + at if k < 2 else core * rows
        copies.append(
            pltpu.make_async_copy(
                wide.at[pl.ds(at, rows)],
                target.at[pl.ds(pl.multiple_of(start, 8), rows)],
                sems.at[k],
            )
        )
        copies[-1].start()
    for copy in copies:
        copy.wait()


def vmem(n):
    return [pl.BlockSpec(memory_space=pltpu.VMEM)] * n


def hbm(n):
    return [pl.BlockSpec(memory_space=pltpu.HBM)] * n


def far(*arrays):
    return [pltpu.with_memory_space_constraint(x, pltpu.HBM) for x in arrays]


LIMIT = 20 * 1024 * 1024


def call(kernel, out, scratch, in_specs, flops, bytes_moved):
    return pl.pallas_call(
        kernel,
        out_shape=tuple(out),
        in_specs=in_specs,
        out_specs=tuple(vmem(len(out))),
        scratch_shapes=scratch,
        cost_estimate=pl.CostEstimate(flops=flops, bytes_accessed=bytes_moved, transcendentals=0),
        compiler_params=pltpu.CompilerParams(vmem_limit_bytes=LIMIT),
    )


def pack_call(pre, og):
    out = [pltpu.VMEM(((CY * CZ + MY * MZ), C1), BF), pltpu.VMEM((CZ + MX * MZ, C1), BF), pltpu.VMEM((CZ + MZ, C1), BF)]
    count = CY + MY + 1 + MX + 2
    return call(pack_kernel, out, [pltpu.SemaphoreType.DMA((count,))], hbm(2), 0, 500_000)(*far(pre, og))


def prep_call(u, pre, og, w1, w2):
    out = [
        pltpu.VMEM((3, 6 * CIN, 2 * C1), BF),
        pltpu.VMEM((9, 2 * C1, 2 * C2), BF),
        pltpu.VMEM((4, 2 * CIN, MX * MY * MZ), BF),
        pltpu.VMEM((4, 2 * C1, CY * CZ), BF),
        pltpu.VMEM(pre.shape, BF),
        pltpu.VMEM(og.shape, BF),
    ]
    scratch = [
        pltpu.VMEM(u.shape, BF),
        pltpu.VMEM(w1.shape, BF),
        pltpu.VMEM(w2.shape, BF),
        pltpu.VMEM((MX * MY * MZ + 8, C1), F32),
        pltpu.SemaphoreType.DMA((5,)),
    ]
    return call(prep_kernel, out, scratch, hbm(5), 0, 6_000_000)(*far(u, pre, og, w1, w2))


def main_call(pre, og, hx, hy, hc, r2, u2t):
    out = [
        pltpu.VMEM((EX * EY * MZ, 2 * C1), BF),
        pltpu.VMEM((ROWS_TWO // 2, C1), BF),
        pltpu.VMEM((ROWS_TWO // 2, C1), BF),
    ]
    scratch = [
        pltpu.VMEM((2 * (CY + 1) * CZ, 2 * C2), BF),
        pltpu.VMEM((EX * EY * MZ + 8, C1), F32),
        pltpu.VMEM((ROWS_TWO, C1), BF),
    ]
    return call(main_kernel, out, scratch, vmem(7), 800_000_000, 4_000_000)(
        pre, og, hx, hy, hc, r2, u2t
    )


def one_call(a, u1t):
    out = [pltpu.VMEM((ROWS_ONE // 2, C1), BF), pltpu.VMEM((ROWS_ONE // 2, C1), BF)]
    scratch = [pltpu.VMEM((ROWS_ONE, C1), BF)]
    return call(one_kernel, out, scratch, vmem(2), 1_200_000_000, 3_000_000)(a, u1t)


def join_call(*parts):
    return call(join_kernel, [pltpu.VMEM((HALF, C1), BF)], [], vmem(4), 0, 2_000_000)(*parts)[0]


def input_call(a, r1):
    out = [jax.ShapeDtypeStruct((1, 2 * MX, 2 * MY, MZ, 2 * CIN), BF)]
    return call(input_kernel, out, [], vmem(2), 1_200_000_000, 3_000_000)(a, r1)[0]


def output_call(half, before=()):
    second = len(before) // 2
    return pl.pallas_call(
        functools.partial(output_kernel, second),
        out_shape=(
            jax.ShapeDtypeStruct((ROWS_ONE, C1), F32),
            jax.ShapeDtypeStruct((ROWS_TWO, C1), F32),
        ),
        in_specs=vmem(1) + hbm(len(before)),
        out_specs=tuple(hbm(2)),
        scratch_shapes=[pltpu.VMEM((HALF, C1), F32), pltpu.SemaphoreType.DMA((3,))],
        input_output_aliases={1: 0, 2: 1} if second else {},
        cost_estimate=pl.CostEstimate(flops=0, bytes_accessed=2_000_000, transcendentals=0),
        compiler_params=pltpu.CompilerParams(vmem_limit_bytes=LIMIT),
        name="output",
    )(half, *before)


def backward(u, pre, og, w1, w2):
    sx = lax.axis_size("y") * lax.axis_size("xl")
    sz = lax.axis_size("zh") * lax.axis_size("zl")
    from_x = [((i + 1) % sx, i) for i in range(sx)]
    from_z = [((i + 1) % sz, i) for i in range(sz)]
    from_xz = [
        ((i + 1) % sx * sz + (j + 1) % sz, i * sz + j) for i in range(sx) for j in range(sz)
    ]
    hx, hy, hc = pack_call(pre, og)
    hx = lax.ppermute(hx, AX, from_x)
    hc = lax.ppermute(hc, AX + AZ, from_xz)
    hy = lax.ppermute(hy, AZ, from_z)
    r1, r2, u1t, u2t, pre, og = prep_call(u, pre, og, w1, w2)
    swap = [(0, 1), (1, 0)]
    a, keep_two, send_two = main_call(pre, og, hx, hy, hc, r2, u2t)
    got_two = lax.ppermute(send_two, "core", swap)
    keep_one, send_one = one_call(a, u1t)
    got_one = lax.ppermute(send_one, "core", swap)
    half = join_call(keep_two, got_two, keep_one, got_one)

    group = ("xh", "xl", "zl", "y")
    parts = lax.all_to_all(half.reshape(GROUP, CHUNK, C1), group, 0, 0, tiled=True)
    grad_input = input_call(a, r1)
    chunk = jnp.sum(parts.astype(F32), axis=0).astype(BF)
    far = lax.ppermute(chunk, "zh", [(i ^ 2, i) for i in range(4)])
    up = lax.ppermute(chunk, "zh", [(i ^ 1, i) for i in range(4)])
    down = lax.ppermute(chunk, "zh", [(i ^ 3, i) for i in range(4)])
    chunk = (chunk.astype(F32) + far.astype(F32)) + (up.astype(F32) + down.astype(F32))
    chunk = jnp.broadcast_to(chunk.astype(BF)[None], (GROUP, CHUNK, C1))
    mine = lax.all_to_all(chunk, group, 0, 0, tiled=True).reshape(HALF, C1)
    other = lax.ppermute(mine, "core", swap)
    grad_one, grad_two = output_call(other, output_call(mine))
    return grad_input, grad_one.reshape(3, 3, 3, CIN, C1), grad_two.reshape(3, 3, 3, C1, C2)


def solution(mesh):
    fine = Mesh(mesh.devices.reshape(2, 2, 4, 2, 4, 2), ("xh", "core", "y", "xl", "zh", "zl"))
    spec = P(("xh", "core"), ("y", "xl"), ("zh", "zl"), None, None)
    return jax.shard_map(
        backward,
        mesh=fine,
        in_specs=(spec, spec, spec, P(), P()),
        out_specs=(spec, P(), P()),
        check_vma=False,
    )
```
